512 devices in a mesh: cube: 128 (over z, y, core), front: 4 (over x).
Axes of the slice: x: 4, y: 4, z: 16, core: 2. Of those that a mesh axis runs over, the one named last changes fastest.
Arguments:
- kkt_blocks: float32 [4, 32768, 128], P('front', 'cube'), may hold values from -1.5 to 1.5
- kkt_owner: int32 [4, 32768, 1], P('front', 'cube'), may hold values from 0 to 127; in each aligned block of 256 rows (0 to 255, 256 to 511, ..., all dimensions but the last counted through in order) at most 4 rows name the same one
- kkt_target: int32 [4, 32768], P('front', 'cube'), may hold values from 0 to 255
- leaf_pivot: float32 [256, 512, 128], P('cube', 'front'), may hold values from -3.5 to 3.5
- pivot_signs: int32 [256, 512], P('cube', 'front'), may hold values from -1 to 1, as said below
- perturb: float32 [256, 512], P('cube', 'front'), may hold values from 0.25 to 1
- leaf_coupling: float32 [256, 512, 128], P('cube', 'front'), may hold values from -1.5 to 1.5
- leaf_map: int32 [256, 512], P('cube', 'front'), may hold values from 256 to 2047
- mid_front: bfloat16 [131072, 2048], P('cube', 'front'), may hold values from -3.5 to 3.5
- level_map: int32 [64, 2048], replicated, may hold values from 256 to 2047, as said below
- top_front: bfloat16 [65536, 2048], P('cube', 'front'), may hold values from -3.5 to 3.5
Outputs:
- leaf_factor: float32 [256, 512, 128], P('cube', 'front')
- mid_factor: float32 [131072, 256], P(('cube', 'front'))
- upper_schur: float32 [65536, 2048], P('cube', 'front')
The draws below stay inside these ranges and needn't reach their ends.
Inputs may be any that keep to these rules, and one draw needn't show every extreme that they name: `kkt_owner`: the rows of one device name one cube index at most 4 times, and some cube index exactly 4 times. `pivot_signs`: every entry is -1 or 1. `level_map`: position p of a level-1 front goes to a position of the same quarter floor(p / 512) of the level-2 front, never below 256.
All inputs are finite; a program needn't handle non-finite values.
Results may differ from the reference program's by a relative error of at most 0.0003.
Values sent between devices are 32-bit elements; how exact they have to be, the bound alone decides.
A program may use at most 64 MiB of HBM per device.

```python
import math
import jax
import jax.numpy as jnp
import numpy as np
from jax import lax

NU = 2048
PIV = 128
RL = 128
PANELS = 2
NS_STEPS = 2
NF = 2
NB = 256
KU = 256
CAP = 4
N_CUBE = 128
N_FRONT = 4


def sign_table(key):
    return 2 * jax.random.randint(jax.random.fold_in(key, 11), (N_CUBE * NF, N_FRONT * PIV), 0, 2) - 1


def draw_pivot_signs(key, part):
    return sign_table(key).astype(jnp.int32)


def draw_leaf_pivot(key, part):
    sign_part = sign_table(key).astype(jnp.float32).reshape(N_CUBE * NF, N_FRONT, PIV)
    key_one, key_two = jax.random.split(jax.random.fold_in(key, 12))
    spread = jax.random.uniform(key_one, sign_part.shape, jnp.float32)
    magnitude = 1.5 + 2.0 * spread
    noise_part = jax.random.uniform(key_two, (N_CUBE * NF, N_FRONT, PIV, PIV), jnp.float32, -1.0, 1.0)
    noise_part = (noise_part + jnp.swapaxes(noise_part, -1, -2)) * (0.25 / math.sqrt(PIV))
    identity = jnp.eye(PIV, dtype=jnp.float32)
    matrix = noise_part * (1.0 - identity) + identity * (sign_part * magnitude)[..., None, :]
    return matrix.reshape(N_CUBE * NF, N_FRONT * PIV, PIV)


def front_entries(key, positions, salt):
    row_count = positions.shape[0]
    key_list = jax.random.split(jax.random.fold_in(key, salt), 4)
    base_part = jnp.clip(jax.random.normal(key_list[0], (row_count, NU), jnp.float32), -4.0, 4.0) * 0.3
    small_part = jax.random.uniform(key_list[1], (row_count, NU), jnp.float32, -1.0, 1.0) * (0.35 / math.sqrt(PIV))
    magnitude = jax.random.uniform(key_list[2], (row_count,), jnp.float32, 1.5, 3.5)
    sign_part = (2 * jax.random.randint(key_list[3], (row_count,), 0, 2) - 1).astype(jnp.float32)
    columns = jnp.arange(NU)
    pivot_area = (positions[:, None] < PANELS * PIV) & (columns[None, :] < PANELS * PIV)
    diagonal = positions[:, None] == columns[None, :]
    values = jnp.where(pivot_area, small_part, base_part)
    values = jnp.where(diagonal & pivot_area, (sign_part * magnitude)[:, None], values)
    return values


def draw_mid_front(key, part):
    positions = jnp.arange(N_CUBE * (NU // 2)) % NU
    return front_entries(key, positions, 21).astype(jnp.bfloat16)


def draw_top_front(key, part):
    all_rows = jnp.arange(N_CUBE * (NU // 4))
    device = all_rows // (NU // 4)
    inner_row = all_rows % (NU // 4)
    row_quarter = 2 * (device % 2) + device // 2 % 2
    positions = row_quarter * (NU // 4) + inner_row
    return front_entries(key, positions, 22).astype(jnp.bfloat16)


def draw_level_map(key, part):
    columns = jnp.broadcast_to(jnp.arange(NU, dtype=jnp.int32), (N_CUBE // 2, NU))
    quarter = columns // (NU // 4)
    lowest = jnp.where(quarter == 0, PANELS * PIV, 0).astype(jnp.int32)
    offset = jax.random.randint(jax.random.fold_in(key, 31), (N_CUBE // 2, NU), lowest, NU // 4)
    return (quarter * (NU // 4) + offset).astype(jnp.int32)


def touch_ends(drawn, own_key, low, largest):
    longest = drawn.shape.index(max(drawn.shape))
    spots = []
    for shift in (0, 1):
        where = [jax.random.randint(jax.random.fold_in(own_key, axis), (), 0, length) for axis, length in enumerate(drawn.shape)]
        where[longest] = (where[longest] + shift) % drawn.shape[longest]
        spots.append(tuple(where))
    return drawn.at[spots[0]].set(low).at[spots[1]].set(largest)


def block_levels(rng, shape, pieces, least, top_value):
    def one(position, parts):
        steps = jax.random.uniform(jax.random.fold_in(jax.random.fold_in(rng, 6), position), (parts,), jnp.float32, least / len(pieces), top_value / len(pieces))
        return jnp.repeat(jnp.exp(steps), shape[position] // parts).reshape((-1,) + (1,) * (len(shape) - position - 1))

    level = one(*pieces[0])
    for cut in pieces[1:]:
        level = level * one(*cut)
    return level


def assign_block(rng, own, number, rows, count, top, limit, skew):
    ranking = jax.random.permutation(rng, count)
    packed, ordinary = portions_of(count, rows * top, limit, skew, True), portions_of(count, rows * top, limit, skew, False)
    places = jnp.arange(count)

    def named(sizes, offset_by):
        used = int((sizes > 0).sum())
        fixed = max(1, used // 4)
        passed = fixed + (places - fixed + offset_by * (used - fixed)) % max(1, count - fixed)
        return jnp.zeros((count,), jnp.int32).at[ranking[jnp.where(places < fixed, places, passed)]].set(jnp.asarray(sizes, jnp.int32))

    sizes = jnp.where(number % 4 == 0, named(packed, number // 4), named(ordinary, number - number // 4 - 1))
    mixed = jax.random.permutation(jax.random.fold_in(own, 3), count)
    giver, taker = mixed[0:count // 2 * 2:2], mixed[1:count // 2 * 2:2]
    slack = jnp.minimum(sizes[giver] - 1, limit - sizes[taker]) // 2
    slack = jnp.where((giver == ranking[0]) | (taker == ranking[0]) | (sizes[taker] == 0), 0, jnp.maximum(slack, 0))
    passed = jax.random.randint(jax.random.fold_in(own, 4), (count // 2,), 0, 1 << 20) % (slack + 1)
    sizes = sizes.at[giver].add(-passed).at[taker].add(passed)
    labels = jnp.searchsorted(jnp.cumsum(sizes), jnp.arange(rows * top), side="right").astype(jnp.int32)
    grid = labels.reshape(top, rows).T
    grid = grid[jax.random.permutation(jax.random.fold_in(own, 1), rows)]
    offset_by = jax.random.randint(jax.random.fold_in(own, 2), (rows, 1), 0, top)
    return jnp.take_along_axis(grid, (jnp.arange(top)[None, :] + offset_by) % top, axis=1)


def portions_of(number_of, total, bound, slope, full):
    weights = [(1 << 20) // math.isqrt(standing ** slope) + 1 for standing in range(1, number_of + 1)]
    largest = bound if full else min(bound, max(-(-total // number_of), total * weights[0] // sum(weights)))
    least = 1 if total - largest >= number_of - 1 else 0
    holding, surplus = [largest] + [least] * (number_of - 1), total - largest - least * (number_of - 1)
    while surplus > 0:
        free = [i for i in range(1, number_of) if holding[i] < largest] or [i for i in range(1, number_of) if holding[i] < bound]
        pool, left = sum([weights[i] for i in free]), surplus
        for i in free:
            more = min(bound - holding[i], max(1, left * weights[i] // pool), surplus)
            holding[i] = holding[i] + more
            surplus = surplus - more
    return np.array(holding)


def bell_draw(key, dims, deviation, limit, cuts=(), kind=jnp.bfloat16):
    entries = deviation * jax.random.normal(key, dims, jnp.float32)
    if cuts:
        entries = entries * block_levels(key, dims, cuts, -0.22, 0.18)
    return jnp.clip(entries, -limit, limit).astype(kind)


def setup_inputs(seed: int = 0) -> dict:
    splits = jax.random.split(jax.random.key(seed), 12)
    kkt_blocks = bell_draw(splits[0], (N_FRONT, N_CUBE * NB, PIV), 0.25, 1.5, ((0, 4), (1, 128)), jnp.float32)
    kkt_owner_keys = jax.random.split(jax.random.fold_in(splits[1], 1), N_FRONT * (N_CUBE * NB) // NB)
    kkt_owner_turns = jax.random.permutation(jax.random.fold_in(splits[1], 3), N_FRONT * (N_CUBE * NB) // NB)
    kkt_owner = jax.vmap(lambda own, number: assign_block(jax.random.fold_in(splits[1], 2), own, number, NB, N_CUBE, 1, CAP, 2))(kkt_owner_keys, kkt_owner_turns).reshape((N_FRONT, N_CUBE * NB, 1))
    kkt_target = touch_ends(jax.random.randint(splits[2], (N_FRONT, N_CUBE * NB), 0, NF * RL), jax.random.fold_in(splits[2], 1), 0, (NF * RL) - 1).astype(jnp.int32)
    leaf_pivot = draw_leaf_pivot(jax.random.fold_in(splits[11], 71), 0)
    pivot_signs = draw_pivot_signs(jax.random.fold_in(splits[11], 71), 0)
    perturb = jnp.clip(jnp.exp(math.log(1.0) - 1.3862944 * jax.random.uniform(splits[5], (N_CUBE * NF, N_FRONT * PIV), jnp.float32) ** block_levels(splits[5], (N_CUBE * NF, N_FRONT * PIV), ((0, 128), (1, 4)), -0.2, 0.2)), 0.25, 1.0)
    leaf_coupling = bell_draw(splits[6], (N_CUBE * NF, N_FRONT * RL, PIV), 0.25, 1.5, ((0, 128), (1, 4)), jnp.float32)
    leaf_map = touch_ends(jax.random.randint(splits[7], (N_CUBE * NF, N_FRONT * RL), KU, NU), jax.random.fold_in(splits[7], 1), KU, NU - 1).astype(jnp.int32)
    mid_front = draw_mid_front(jax.random.fold_in(splits[11], 71), 0)
    level_map = draw_level_map(jax.random.fold_in(splits[11], 71), 0)
    top_front = draw_top_front(jax.random.fold_in(splits[11], 71), 0)
    return {"kkt_blocks": kkt_blocks, "kkt_owner": kkt_owner, "kkt_target": kkt_target, "leaf_pivot": leaf_pivot, "pivot_signs": pivot_signs, "perturb": perturb, "leaf_coupling": leaf_coupling, "leaf_map": leaf_map, "mid_front": mid_front, "level_map": level_map, "top_front": top_front}


HIGHEST = lax.Precision.HIGHEST


def newton_inverse(pivot_block):
    diagonal = jnp.diagonal(pivot_block, axis1=-2, axis2=-1)
    current = jnp.eye(pivot_block.shape[-1], dtype=jnp.float32) * (1.0 / diagonal)[..., None, :]
    for sweep_index in range(NS_STEPS):
        product = jnp.einsum("...ij,...jk->...ik", pivot_block, current, precision=HIGHEST)
        current = 2.0 * current - jnp.einsum("...ij,...jk->...ik", current, product, precision=HIGHEST)
    return current


def eliminate(front_matrix):
    positions = jnp.arange(NU)
    factors = []
    for panel_index in range(PANELS):
        first_col = panel_index * PIV
        finish = first_col + PIV
        columns = front_matrix[:, first_col:finish]
        inverse = newton_inverse(columns[first_col:finish])
        keep_rows = (positions >= finish).astype(jnp.float32)[:, None]
        lower_rows = jnp.dot(columns, inverse, precision=HIGHEST) * keep_rows
        front_matrix = front_matrix - jnp.dot(lower_rows, (columns * keep_rows).T, precision=HIGHEST)
        factors.append(lower_rows)
    return front_matrix, jnp.concatenate(factors, axis=1)


def one_group(inputs):
    leaf_terms, leaf_maps, mid_parts, level_links, top_part = inputs
    positions = jnp.arange(NU)
    kept_rows = positions >= PANELS * PIV
    link_terms = []
    link_ids = []
    factors = []
    for child_index in range(2):
        mapping = leaf_maps[child_index]
        flat_index = mapping[..., :, None] * NU + mapping[..., None, :]
        assembled = jax.ops.segment_sum(leaf_terms[child_index].reshape(-1), flat_index.reshape(-1), num_segments=NU * NU)
        schur_part, lower_rows = eliminate(mid_parts[child_index].astype(jnp.float32) + assembled.reshape(NU, NU))
        factors.append(lower_rows)
        links = level_links[child_index]
        pair_ids = jnp.where(kept_rows[:, None] & kept_rows[None, :], links[:, None] * NU + links[None, :], NU * NU)
        link_ids.append(pair_ids.reshape(-1))
        link_terms.append(schur_part.reshape(-1))
    top_added = jax.ops.segment_sum(jnp.concatenate(link_terms), jnp.concatenate(link_ids), num_segments=NU * NU + 1)[:-1]
    final_front, unused = eliminate(top_part.astype(jnp.float32) + top_added.reshape(NU, NU))
    return final_front, jnp.stack(factors)


def reference(kkt_blocks, kkt_owner, kkt_target, leaf_pivot, pivot_signs, perturb, leaf_coupling, leaf_map, mid_front, level_map, top_front):
    owner_index = kkt_owner[:, :, 0]
    front_index = jnp.arange(N_FRONT, dtype=jnp.int32)[:, None]
    flat_rows = (owner_index * NF + kkt_target // RL) * (N_FRONT * RL) + front_index * RL + kkt_target % RL
    arrivals = jax.ops.segment_sum(kkt_blocks.reshape(-1, PIV), flat_rows.reshape(-1), num_segments=N_CUBE * NF * N_FRONT * RL)
    coupling = (leaf_coupling + arrivals.reshape(N_CUBE * NF, N_FRONT * RL, PIV)).reshape(N_CUBE * NF, N_FRONT, RL, PIV)
    identity = jnp.eye(PIV, dtype=jnp.float32)
    shifts = (pivot_signs.astype(jnp.float32) * perturb).reshape(N_CUBE * NF, N_FRONT, PIV)
    pivots = leaf_pivot.reshape(N_CUBE * NF, N_FRONT, PIV, PIV) + identity * shifts[..., None, :]
    inverse = newton_inverse(pivots)
    factor = jnp.einsum("lfrk,lfkj->lfrj", coupling, inverse, precision=HIGHEST)
    contrib = -jnp.einsum("lfrk,lfsk->lfrs", factor, coupling, precision=HIGHEST)
    groups = N_CUBE // 4
    leaf_terms = contrib.reshape(groups, 2, 2, NF, N_FRONT, RL, RL)
    leaf_maps = leaf_map.reshape(groups, 2, 2, NF, N_FRONT, RL)
    mid_parts = mid_front.reshape(groups, 2, NU, NU)
    level_links = level_map.reshape(groups, 2, NU)
    top_parts = jnp.transpose(top_front.reshape(groups, 2, 2, NU // 4, NU), (0, 2, 1, 3, 4)).reshape(groups, NU, NU)
    finals, mid_factors = lax.map(one_group, (leaf_terms, leaf_maps, mid_parts, level_links, top_parts))
    upper_schur = jnp.transpose(finals.reshape(groups, 2, 2, NU // 4, NU), (0, 2, 1, 3, 4)).reshape(N_CUBE * NU // 4, NU)
    mid_factor = mid_factors.reshape(N_CUBE * NU // 2, PANELS * PIV)
    leaf_factor = factor.reshape(N_CUBE * NF, N_FRONT * RL, PIV)
    return leaf_factor, mid_factor, upper_schur
```

```python
import functools

import jax
import jax.numpy as jnp
from jax import lax
from jax.experimental import pallas as pl
from jax.experimental.pallas import tpu as pltpu
from jax.sharding import PartitionSpec as P

PIV = 128
QUARTER = 512
PLANE = 8
SLOTS = 40
CHUNKS = 12
F32 = jnp.float32
BF16 = jnp.bfloat16
MESH = pl.DeviceIdType.MESH
NN = (((1,), (0,)), ((), ()))
NT = (((1,), (1,)), ((), ()))


def mm(a, b, dims=NN):
    return lax.dot_general(a, b, dims, preferred_element_type=F32)


def exact(a, b, dims=NN):
    return lax.dot_general(
        a, b, dims, precision=lax.Precision.HIGHEST, preferred_element_type=F32
    )


def halves(a):
    high = a.astype(BF16)
    return high, (a - high.astype(F32)).astype(BF16)


def dot3(a, b, dims=NN):
    a_high, a_low = halves(a)
    b_high, b_low = halves(b)
    return mm(a_high, b_high, dims) + (mm(a_high, b_low, dims) + mm(a_low, b_high, dims))


def iota(shape, axis):
    return lax.broadcasted_iota(jnp.int32, shape, axis)


def hits(a, b):
    return jnp.where(a == b, 1.0, 0.0).astype(BF16)


def newton_inverse(block):
    eye = iota((PIV, PIV), 0) == iota((PIV, PIV), 1)
    on_diagonal = jnp.where(eye, block, 0.0)
    by_col = 1.0 / jnp.sum(on_diagonal, axis=0, keepdims=True)
    by_row = 1.0 / jnp.sum(on_diagonal, axis=1, keepdims=True)
    current = jnp.where(eye, 2.0 * by_col, 0.0) - by_row * (block * by_col)
    return 2.0 * current - exact(current, exact(block, current))


def fused(
    depth_z,
    blocks,
    owner,
    target,
    leaf_pivot,
    signs,
    perturb,
    leaf_coupling,
    leaf_map,
    mid,
    level,
    top,
    factor_out,
    mid_factor_out,
    upper_out,
    s1,
    r1,
    s2,
    r2,
    rbuf,
    piv,
    inv_sets,
    leaf_inv,
    lfull,
    l_high,
    l_low,
    p_high,
    p_low,
    vout,
    vin,
    kb,
    rt,
    kr_high,
    kr_low,
    zs,
    zr,
    ds,
    dr,
    ps,
    pr,
    es,
    er,
    vs,
    vr,
    ks,
    kr,
):
    cube = lax.axis_index("cube")
    front = lax.axis_index("front")
    pos_z = cube // PLANE
    pos_d = cube % PLANE
    low = cube % 2
    high = (cube // 2) % 2
    rho = 2 * low + high
    core_peer = cube + 1 - 2 * low
    y_peer = cube + 2 - 4 * high
    both_peer = core_peer + 2 - 4 * high
    plane_base = cube - pos_d
    group = cube // 2
    row_count = blocks.shape[1]
    cube_count = depth_z * PLANE

    def at_z(step):
        return (pos_z + step) % depth_z

    def at_plane(step):
        return (pos_d + step) % PLANE

    barrier = pltpu.get_barrier_semaphore()

    def greet_z(step, carry):
        pl.semaphore_signal(
            barrier, inc=1, device_id=(at_z(step) * PLANE + pos_d, front), device_id_type=MESH
        )
        return carry

    def greet_plane(step, carry):
        pl.semaphore_signal(
            barrier, inc=1, device_id=(plane_base + at_plane(step), front), device_id_type=MESH
        )
        return carry

    lax.fori_loop(1, depth_z, greet_z, 0)
    lax.fori_loop(1, PLANE, greet_plane, 0)
    for step in range(1, 4):
        pl.semaphore_signal(
            barrier, inc=1, device_id=(cube, (front + step) % 4), device_id_type=MESH
        )

    @pl.when(front == 0)
    def _():
        rbuf[0:1024, :] = mid[:, 0:256].astype(F32)
        rbuf[1536:2048, :] = top[:, 0:256].astype(F32)

    own = owner[...]
    own_mask = iota((cube_count, row_count), 0) == own
    own_hits = jnp.where(own_mask, 1.0, 0.0).astype(BF16)
    before = jnp.where(
        iota((row_count, row_count), 0) < iota((row_count, row_count), 1), 1.0, 0.0
    ).astype(BF16)
    ahead = mm(own_hits, before)
    rank = jnp.sum(jnp.where(own_mask, ahead, 0.0), axis=0, keepdims=True).astype(jnp.int32)
    base = (own >> 3) * SLOTS + (own & 7)
    send_rows = depth_z * SLOTS
    row_ids = iota((send_rows, row_count), 0)
    to_slot = hits(row_ids, base + rank * PLANE)
    value_high, value_low = halves(blocks[0])
    marks = jnp.where(row_ids == base + 32, (target[...] + 1).astype(F32), 0.0).astype(BF16)
    by_rank = hits(iota((PIV, row_count), 0), rank)
    s1[...] = mm(to_slot, value_high) + mm(to_slot, value_low) + mm(marks, by_rank, NT)

    pl.semaphore_wait(barrier, depth_z + PLANE + 1)

    def z_copy(step):
        there = at_z(step)
        return pltpu.make_async_remote_copy(
            src_ref=s1.at[pl.ds(pl.multiple_of(there * SLOTS, 8), SLOTS)],
            dst_ref=r1.at[pl.ds(pl.multiple_of(pos_z * SLOTS, 8), SLOTS)],
            send_sem=zs.at[step],
            recv_sem=zr.at[step],
            device_id=(there * PLANE + pos_d, front),
            device_id_type=MESH,
        )

    def start_z(step, carry):
        z_copy(step).start()
        return carry

    lax.fori_loop(1, depth_z, start_z, 0)

    def chunk_copy(index, there):
        rows = pl.ds(pl.multiple_of(index * PIV + 512 * (index // 8), PIV), PIV)
        return pltpu.make_async_remote_copy(
            src_ref=rbuf.at[rows],
            dst_ref=rbuf.at[rows],
            send_sem=ps.at[index],
            recv_sem=pr.at[index],
            device_id=(cube, there),
            device_id_type=MESH,
        )

    up = (front + 1) % 4
    down = (front + 3) % 4

    @pl.when(front == 0)
    def _():
        def push(index, carry):
            chunk_copy(index, up).start()
            chunk_copy(index + 6, down).start()
            return carry

        lax.fori_loop(0, 6, push, 0)

    own_rows = pl.ds(pl.multiple_of(pos_z * SLOTS, 8), SLOTS)
    r1[own_rows, :] = s1[own_rows, :]

    eye = iota((PIV, PIV), 0) == iota((PIV, PIV), 1)
    links = level[pl.ds(group, 1), :]
    two_rows = iota((16, 2048), 0)
    digits = jnp.where(two_rows == 0, links >> 4, jnp.where(two_rows == 1, links & 15, 0))
    digits = digits.astype(F32).astype(BF16)

    def prepare_leaf(leaf, carry):
        shift = signs[pl.ds(leaf, 1), :].astype(F32) * perturb[pl.ds(leaf, 1), :]
        leaf_inv[leaf] = newton_inverse(leaf_pivot[leaf] + jnp.where(eye, shift, 0.0))
        picked = mm(digits, hits(iota((2048, PIV), 0), leaf_map[pl.ds(leaf, 1), :]))
        composite = picked[0:1, :] * 16.0 + picked[1:2, :]
        kb[0, front, leaf, 128:136, :] = jnp.broadcast_to(composite, (8, PIV))
        return carry

    lax.fori_loop(0, 2, prepare_leaf, 0)

    @pl.when(front != 0)
    def _():
        def forward(index, carry):
            chunk_copy(index, up).wait_recv()

            @pl.when(front != 3)
            def _():
                chunk_copy(index, up).start()

            chunk_copy(index + 6, down).wait_recv()

            @pl.when(front != 1)
            def _():
                chunk_copy(index + 6, down).start()

            return carry

        lax.fori_loop(0, 6, forward, 0)

    col_g = pl.ds(1024, 512)
    col_u = pl.ds(2048, 512)
    holds_g = low == front // 2
    holds_u = rho == front
    first_g = pl.ds(pl.multiple_of((front % 2) * 512, 512), 512)
    pivot_g = pl.ds(0, 256)
    pivot_u = pl.ds(1536, 256)
    whole_u = pl.ds(1536, 512)
    peers = (core_peer, y_peer, both_peer)

    def edge(source, place, number, arrival, there):
        return pltpu.make_async_remote_copy(
            src_ref=source,
            dst_ref=place,
            send_sem=es.at[number],
            recv_sem=er.at[arrival],
            device_id=(there, front),
            device_id_type=MESH,
        )

    def edges_g():
        return edge(rbuf.at[first_g], rbuf.at[col_g], 0, 0, core_peer)

    def edges_pg():
        return edge(rbuf.at[pivot_g], piv.at[0], 1, 1, core_peer)

    def edges_u(which):
        return edge(rbuf.at[whole_u], rbuf.at[col_u], 2 + which, 2, peers[which])

    def edges_pu(which):
        return edge(rbuf.at[pivot_u], piv.at[1], 5 + which, 3, peers[which])

    @pl.when(low == 0)
    def _():
        edges_pg().start()
        piv[0] = rbuf[pivot_g, :]

    @pl.when(rho == 0)
    def _():
        for which in range(3):
            edges_pu(which).start()
        piv[1] = rbuf[pivot_u, :]

    @pl.when(holds_g)
    def _():
        edges_g().start()
        rbuf[col_g, :] = rbuf[first_g, :]

    @pl.when(holds_u)
    def _():
        for which in range(3):
            edges_u(which).start()
        rbuf[col_u, :] = rbuf[whole_u, :]

    def wait_z(step, carry):
        z_copy(step).wait_recv()
        return carry

    lax.fori_loop(1, depth_z, wait_z, 0)
    for place in range(PLANE):
        for slot in range(5):
            s2[place, slot] = r1[pl.ds(slot * PLANE + place, depth_z, stride=SLOTS), :]

    def d_copy(step):
        there = at_plane(step)
        return pltpu.make_async_remote_copy(
            src_ref=s2.at[there],
            dst_ref=r2.at[pos_d],
            send_sem=ds.at[step],
            recv_sem=dr.at[step],
            device_id=(plane_base + there, front),
            device_id_type=MESH,
        )

    def start_d(step, carry):
        d_copy(step).start()
        return carry

    lax.fori_loop(1, PLANE, start_d, 0)
    r2[pos_d] = s2[pos_d]

    @pl.when(low != 0)
    def _():
        edges_pg().wait_recv()

    @pl.when(rho != 0)
    def _():
        edges_pu(0).wait_recv()

    def invert_set(number, carry):
        rows_two = piv[number, 128:256, 0:128]
        first = newton_inverse(piv[number, 0:128, 0:128])
        second = newton_inverse(
            piv[number, 128:256, 128:256] - exact(exact(rows_two, first), rows_two, NT)
        )
        inv_sets[number, 0] = first
        inv_sets[number, 1] = second
        inv_sets[number, 2] = rows_two
        return carry

    lax.fori_loop(0, 2, invert_set, 0)

    def wait_d(step, carry):
        d_copy(step).wait_recv()
        return carry

    lax.fori_loop(1, PLANE, wait_d, 0)

    slots_per = PLANE * depth_z
    marks_in = r2[:, 4].reshape(slots_per, PIV).T.astype(jnp.int32)
    arrivals = jnp.zeros((256, PIV), F32)
    for slot in range(4):
        to_row = hits(iota((256, slots_per), 0) + 1, marks_in[slot : slot + 1, :])
        got_high, got_low = halves(r2[:, slot].reshape(slots_per, PIV))
        arrivals = arrivals + mm(to_row, got_high) + mm(to_row, got_low)
    for leaf in range(2):
        coupling = leaf_coupling[leaf] + arrivals[leaf * PIV : (leaf + 1) * PIV, :]
        factor = exact(coupling, leaf_inv[leaf])
        factor_out[leaf] = factor
        kb[0, front, leaf, 0:128, :] = -exact(factor, coupling, NT)

    def k_copy(source, place, where, send, arrival, there):
        return pltpu.make_async_remote_copy(
            src_ref=kb.at[source, where],
            dst_ref=kb.at[place, where],
            send_sem=ks.at[send],
            recv_sem=kr.at[arrival],
            device_id=there,
            device_id_type=MESH,
        )

    def k_y():
        return k_copy(0, 2, front, 0, 0, (y_peer, front))

    def k_front(which, step):
        number = 1 + 3 * which + step - 1
        return k_copy(
            2 * which, 2 * which, front, number, number, (cube, (front + step) % 4)
        )

    def k_core(which, step):
        number = 7 + 4 * which + step
        return k_copy(
            2 * which,
            2 * which + 1,
            (front + 4 - step) % 4,
            number,
            number,
            (core_peer, front),
        )

    k_y().start()
    for step in (1, 3, 2):
        k_front(0, step).start()
    k_core(0, 0).start()

    @pl.when(low != front // 2)
    def _():
        edges_g().wait_recv()

    def panel(index, carry):
        number = index // 3
        start = jnp.where(
            index < 2,
            low * 1024 + index * 512,
            jnp.where(index == 3, rho * 512, front * 512),
        )
        rows = pl.ds(pl.multiple_of(index * 512, 512), 512)
        place = iota((512, PIV), 0) + start
        first = rbuf[rows, 0:128]
        second = rbuf[rows, 128:256]
        past_one = place >= 128
        past_two = place >= 256
        lower_one = jnp.where(past_one, dot3(first, inv_sets[number, 0]), 0.0)
        second = second - dot3(lower_one, inv_sets[number, 2], NT)
        lower_two = jnp.where(past_two, dot3(second, inv_sets[number, 1]), 0.0)
        lfull[rows, 0:128] = lower_one
        lfull[rows, 128:256] = lower_two
        one_high, one_low = halves(lower_one)
        two_high, two_low = halves(lower_two)
        l_high[rows, 0:128] = one_high
        l_high[rows, 128:256] = two_high
        l_low[rows, 0:128] = one_low
        l_low[rows, 128:256] = two_low
        one_high, one_low = halves(jnp.where(past_one, first, 0.0))
        two_high, two_low = halves(jnp.where(past_two, second, 0.0))
        p_high[rows, 0:128] = one_high
        p_high[rows, 128:256] = two_high
        p_low[rows, 0:128] = one_low
        p_low[rows, 128:256] = two_low
        return carry

    lax.fori_loop(0, 3, panel, 0)

    def update(l_rows, p_rows):
        return mm(l_high[l_rows, :], p_high[p_rows, :], NT) + (
            mm(l_high[l_rows, :], p_low[p_rows, :], NT)
            + mm(l_low[l_rows, :], p_high[p_rows, :], NT)
        )

    def quarter_map(quarter):
        entries = level[pl.ds(group, 1), pl.ds(pl.multiple_of(quarter * 512, 512), 512)]
        kept = iota((1, 512), 1) + quarter * 512 >= 256
        return hits(iota((512, 512), 0), jnp.where(kept, entries - quarter * 512, -1))

    col_hits = quarter_map(front)

    def link(turn, carry):
        half = turn * high + (1 - turn) * (1 - high)
        rows = pl.ds(pl.multiple_of(half * 512, 512), 512)
        schur = mid[rows, :].astype(F32) - update(rows, col_g)
        s_high, s_low = halves(schur)
        t_high, t_low = halves(mm(s_high, col_hits, NT) + mm(s_low, col_hits, NT))
        row_hits = quarter_map(2 * low + half)
        vout[turn] = mm(row_hits, t_high) + mm(row_hits, t_low)
        return carry

    def v_copy():
        return pltpu.make_async_remote_copy(
            src_ref=vout.at[0],
            dst_ref=vin,
            send_sem=vs.at[0],
            recv_sem=vr.at[0],
            device_id=(y_peer, front),
            device_id_type=MESH,
        )

    k_y().wait_recv()
    for step in (1, 3, 2):
        k_front(1, step).start()
    k_core(1, 0).start()
    lax.fori_loop(0, 1, link, 0)
    v_copy().start()
    lax.fori_loop(1, 2, link, 0)

    @pl.when(rho != front)
    def _():
        edges_u(0).wait_recv()

    lax.fori_loop(3, 5, panel, 0)
    mid_factor_out[...] = lfull[pl.ds(pl.multiple_of(front * 256, 256), 256), :]
    upper_out[...] = top[...].astype(F32) - update(whole_u, col_u) + vout[1]

    ids = iota((512, PIV), 0)

    def gather_group(which, carry):
        def one(index, inner):
            entry = index // 2
            leaf = index % 2
            composite = kb[which, entry, leaf, 128:129, :].astype(jnp.int32)
            cols = pl.ds(pl.multiple_of(index * PIV, PIV), PIV)
            rt[:, cols] = hits(ids, composite - rho * 512)
            col_ids = hits(ids, composite - front * 512)
            k_high, k_low = halves(kb[which, entry, leaf, 0:128, :])
            spread_high, spread_low = halves(mm(k_high, col_ids, NT) + mm(k_low, col_ids, NT))
            kr_high[cols, :] = spread_high
            kr_low[cols, :] = spread_low
            return inner

        lax.fori_loop(0, 8, one, 0)
        upper_out[...] += mm(rt[...], kr_high[...]) + mm(rt[...], kr_low[...])
        return carry

    for step in (1, 3, 2):
        k_front(0, step).wait_recv()
        k_core(0, step).start()
        k_front(1, step).wait_recv()
        k_core(1, step).start()
    lax.fori_loop(0, 2, lambda turn, carry: gather_group(2 * turn, carry), 0)
    v_copy().wait_recv()
    upper_out[...] += vin[...]
    for step in range(4):
        k_core(0, step).wait_recv()
        k_core(1, step).wait_recv()
    lax.fori_loop(0, 2, lambda turn, carry: gather_group(2 * turn + 1, carry), 0)

    def end_z(step, carry):
        z_copy(step).wait_send()
        return carry

    def end_d(step, carry):
        d_copy(step).wait_send()
        return carry

    lax.fori_loop(1, depth_z, end_z, 0)
    lax.fori_loop(1, PLANE, end_d, 0)

    @pl.when(front != 3)
    def _():
        def end_up(index, carry):
            chunk_copy(index, up).wait_send()
            return carry

        lax.fori_loop(0, 6, end_up, 0)

    @pl.when(front != 1)
    def _():
        def end_down(index, carry):
            chunk_copy(index, down).wait_send()
            return carry

        lax.fori_loop(6, 12, end_down, 0)

    @pl.when(low == 0)
    def _():
        edges_pg().wait_send()

    @pl.when(holds_g)
    def _():
        edges_g().wait_send()

    @pl.when(rho == 0)
    def _():
        for which in range(3):
            edges_pu(which).wait_send()

    @pl.when(holds_u)
    def _():
        for which in range(3):
            edges_u(which).wait_send()

    v_copy().wait_send()
    k_y().wait_send()
    for which in range(2):
        for step in range(1, 4):
            k_front(which, step).wait_send()
        for step in range(4):
            k_core(which, step).wait_send()


def local(
    kkt_blocks,
    kkt_owner,
    kkt_target,
    leaf_pivot,
    pivot_signs,
    perturb,
    leaf_coupling,
    leaf_map,
    mid_front,
    level_map,
    top_front,
):
    depth_z = lax.axis_size("cube") // PLANE
    vmem = pl.BlockSpec(memory_space=pltpu.VMEM)
    dma = pltpu.SemaphoreType.DMA
    return pl.pallas_call(
        functools.partial(fused, depth_z),
        out_shape=(
            jax.ShapeDtypeStruct((2, PIV, PIV), F32),
            jax.ShapeDtypeStruct((256, 256), F32),
            jax.ShapeDtypeStruct((512, 512), F32),
        ),
        in_specs=[vmem] * 11,
        out_specs=(vmem, vmem, vmem),
        scratch_shapes=[
            pltpu.VMEM((depth_z * SLOTS, PIV), F32),
            pltpu.VMEM((depth_z * SLOTS, PIV), F32),
            pltpu.VMEM((PLANE, 5, depth_z, PIV), F32),
            pltpu.VMEM((PLANE, 5, depth_z, PIV), F32),
            pltpu.VMEM((2560, 256), F32),
            pltpu.VMEM((2, 256, 256), F32),
            pltpu.VMEM((2, 3, PIV, PIV), F32),
            pltpu.VMEM((2, PIV, PIV), F32),
            pltpu.VMEM((2560, 256), F32),
            pltpu.VMEM((2560, 256), BF16),
            pltpu.VMEM((2560, 256), BF16),
            pltpu.VMEM((2560, 256), BF16),
            pltpu.VMEM((2560, 256), BF16),
            pltpu.VMEM((2, 512, 512), F32),
            pltpu.VMEM((512, 512), F32),
            pltpu.VMEM((4, 4, 2, 136, PIV), F32),
            pltpu.VMEM((512, 1024), BF16),
            pltpu.VMEM((1024, 512), BF16),
            pltpu.VMEM((1024, 512), BF16),
            dma((depth_z,)),
            dma((depth_z,)),
            dma((PLANE,)),
            dma((PLANE,)),
            dma((CHUNKS,)),
            dma((CHUNKS,)),
            dma((8,)),
            dma((4,)),
            dma((1,)),
            dma((1,)),
            dma((15,)),
            dma((15,)),
        ],
        compiler_params=pltpu.CompilerParams(
            collective_id=0, has_side_effects=True, vmem_limit_bytes=56 * 1024 * 1024
        ),
    )(
        kkt_blocks,
        kkt_owner.reshape(1, -1),
        kkt_target,
        leaf_pivot,
        pivot_signs,
        perturb,
        leaf_coupling,
        leaf_map,
        mid_front,
        level_map,
        top_front,
    )


def solution(mesh):
    in_specs = (
        P("front", "cube", None),
        P("front", "cube", None),
        P("front", "cube"),
        P("cube", "front", None),
        P("cube", "front"),
        P("cube", "front"),
        P("cube", "front", None),
        P("cube", "front"),
        P("cube", "front"),
        P(),
        P("cube", "front"),
    )
    out_specs = (P("cube", "front", None), P(("cube", "front"), None), P("cube", "front"))
    return jax.shard_map(local, mesh=mesh, in_specs=in_specs, out_specs=out_specs, check_vma=False)
```

```python
import functools

import jax
import jax.numpy as jnp
from jax import lax
from jax.experimental import pallas as pl
from jax.experimental.pallas import tpu as pltpu
from jax.sharding import PartitionSpec as P

PIV = 128
QUARTER = 512
PLANE = 8
SLOTS = 40
CHUNK = 32
HALF = 16
F32 = jnp.float32
BF16 = jnp.bfloat16
MESH = pl.DeviceIdType.MESH
NN = (((1,), (0,)), ((), ()))
NT = (((1,), (1,)), ((), ()))


def mm(a, b, dims=NN):
    return lax.dot_general(a, b, dims, preferred_element_type=F32)


def exact(a, b, dims=NN):
    return lax.dot_general(
        a, b, dims, precision=lax.Precision.HIGHEST, preferred_element_type=F32
    )


def halves(a):
    high = a.astype(BF16)
    return high, (a - high.astype(F32)).astype(BF16)


def dot3(a, b, dims=NN):
    a_high, a_low = halves(a)
    b_high, b_low = halves(b)
    return mm(a_high, b_high, dims) + (mm(a_high, b_low, dims) + mm(a_low, b_high, dims))


def iota(shape, axis):
    return lax.broadcasted_iota(jnp.int32, shape, axis)


def hits(a, b):
    return jnp.where(a == b, 1.0, 0.0).astype(BF16)


def newton_inverse(block):
    eye = iota((PIV, PIV), 0) == iota((PIV, PIV), 1)
    on_diagonal = jnp.where(eye, block, 0.0)
    by_col = 1.0 / jnp.sum(on_diagonal, axis=0, keepdims=True)
    by_row = 1.0 / jnp.sum(on_diagonal, axis=1, keepdims=True)
    current = jnp.where(eye, 2.0 * by_col, 0.0) - by_row * (block * by_col)
    return 2.0 * current - exact(current, exact(block, current))


def fused(
    depth_z,
    blocks,
    owner,
    target,
    leaf_pivot,
    signs,
    perturb,
    leaf_coupling,
    leaf_map,
    mid,
    level,
    top,
    factor_out,
    mid_factor_out,
    upper_out,
    s1,
    r1,
    s2,
    r2,
    rbuf,
    relay,
    piv,
    inv_sets,
    leaf_inv,
    lfull,
    l_high,
    l_low,
    p_high,
    p_low,
    vout,
    vin,
    kb,
    rt,
    kr_high,
    kr_low,
    zs,
    zr,
    ds,
    dr,
    ps,
    pr,
    gs,
    gr,
    hs,
    hr,
    us,
    ur,
    es,
    er,
    xs,
    xr,
    vs,
    vr,
    ks,
    kr,
):
    cube = lax.axis_index("cube")
    front = lax.axis_index("front")
    pos_z = cube // PLANE
    pos_d = cube % PLANE
    low = cube % 2
    high = (cube // 2) % 2
    rho = 2 * low + high
    core_peer = cube + 1 - 2 * low
    y_peer = cube + 2 - 4 * high
    plane_base = cube - pos_d
    group = cube // 2
    row_count = blocks.shape[1]
    cube_count = depth_z * PLANE

    def at_z(step):
        return (pos_z + step) % depth_z

    def at_plane(step):
        return (pos_d + step) % PLANE

    barrier = pltpu.get_barrier_semaphore()

    def greet_z(step, carry):
        pl.semaphore_signal(
            barrier, inc=1, device_id=(at_z(step) * PLANE + pos_d, front), device_id_type=MESH
        )
        return carry

    def greet_plane(step, carry):
        pl.semaphore_signal(
            barrier, inc=1, device_id=(plane_base + at_plane(step), front), device_id_type=MESH
        )
        return carry

    lax.fori_loop(1, depth_z, greet_z, 0)
    lax.fori_loop(1, PLANE, greet_plane, 0)
    for step in range(1, 4):
        pl.semaphore_signal(
            barrier, inc=1, device_id=(cube, (front + step) % 4), device_id_type=MESH
        )

    @pl.when(front == 0)
    def _():
        rbuf[0:1024, :] = mid[:, 0:256].astype(F32)
        rbuf[1536:2048, :] = top[:, 0:256].astype(F32)

    own = owner[...]
    own_mask = iota((cube_count, row_count), 0) == own
    own_hits = jnp.where(own_mask, 1.0, 0.0).astype(BF16)
    before = jnp.where(
        iota((row_count, row_count), 0) < iota((row_count, row_count), 1), 1.0, 0.0
    ).astype(BF16)
    ahead = mm(own_hits, before)
    rank = jnp.sum(jnp.where(own_mask, ahead, 0.0), axis=0, keepdims=True).astype(jnp.int32)
    base = (own >> 3) * SLOTS + (own & 7)
    send_rows = depth_z * SLOTS
    row_ids = iota((send_rows, row_count), 0)
    to_slot = hits(row_ids, base + rank * PLANE)
    value_high, value_low = halves(blocks[0])
    marks = jnp.where(row_ids == base + 32, (target[...] + 1).astype(F32), 0.0).astype(BF16)
    by_rank = hits(iota((PIV, row_count), 0), rank)
    s1[...] = mm(to_slot, value_high) + mm(to_slot, value_low) + mm(marks, by_rank, NT)

    pl.semaphore_wait(barrier, depth_z + PLANE + 1)

    def z_copy(step):
        there = at_z(step)
        return pltpu.make_async_remote_copy(
            src_ref=s1.at[pl.ds(pl.multiple_of(there * SLOTS, 8), SLOTS)],
            dst_ref=r1.at[pl.ds(pl.multiple_of(pos_z * SLOTS, 8), SLOTS)],
            send_sem=zs.at[step],
            recv_sem=zr.at[step],
            device_id=(there * PLANE + pos_d, front),
            device_id_type=MESH,
        )

    def start_z(step, carry):
        z_copy(step).start()
        return carry

    lax.fori_loop(1, depth_z, start_z, 0)

    def chunk_copy(index, there):
        rows = pl.ds(pl.multiple_of(index * CHUNK, CHUNK), CHUNK)
        return pltpu.make_async_remote_copy(
            src_ref=rbuf.at[rows],
            dst_ref=rbuf.at[rows],
            send_sem=ps.at[index],
            recv_sem=pr.at[index],
            device_id=(cube, there),
            device_id_type=MESH,
        )

    up = (front + 1) % 4
    down = (front + 3) % 4
    holds_g = low == front // 2
    holds_u = rho == front
    col_g = pl.ds(1024, 512)
    col_u = pl.ds(2048, 512)
    first_g = pl.ds(pl.multiple_of((front % 2) * 512, 512), 512)
    pivot_g = pl.ds(0, 256)
    pivot_u = pl.ds(1536, 256)
    whole_u = pl.ds(1536, 512)

    def col_copy(part):
        start = (front % 2) * 512 + part * CHUNK
        return pltpu.make_async_remote_copy(
            src_ref=rbuf.at[pl.ds(pl.multiple_of(start, CHUNK), CHUNK)],
            dst_ref=rbuf.at[pl.ds(pl.multiple_of(1024 + part * CHUNK, CHUNK), CHUNK)],
            send_sem=gs.at[part],
            recv_sem=gr.at[part],
            device_id=(core_peer, front),
            device_id_type=MESH,
        )

    def pivot_copy(part):
        rows = pl.ds(pl.multiple_of(part * CHUNK, CHUNK), CHUNK)
        return pltpu.make_async_remote_copy(
            src_ref=rbuf.at[rows],
            dst_ref=piv.at[0, rows],
            send_sem=hs.at[part],
            recv_sem=hr.at[part],
            device_id=(core_peer, front),
            device_id_type=MESH,
        )

    def landed(index):
        @pl.when((low == 0) & (index < 8))
        def _():
            pivot_copy(index).start()

        @pl.when(holds_g & (index // HALF == front % 2))
        def _():
            col_copy(index % HALF).start()

    def upper_copy(half, there, number):
        rows = pl.ds(pl.multiple_of(1536 + 256 * half, 256), 256)
        return pltpu.make_async_remote_copy(
            src_ref=rbuf.at[rows],
            dst_ref=rbuf.at[rows],
            send_sem=us.at[number],
            recv_sem=ur.at[half],
            device_id=(cube, there),
            device_id_type=MESH,
        )

    def edge(source, place, number, arrival, there):
        return pltpu.make_async_remote_copy(
            src_ref=source,
            dst_ref=place,
            send_sem=es.at[number],
            recv_sem=er.at[arrival],
            device_id=(there, front),
            device_id_type=MESH,
        )

    def edge_col(number, there):
        return edge(rbuf.at[whole_u], rbuf.at[col_u], number, 0, there)

    def edge_col_on():
        return edge(rbuf.at[col_u], rbuf.at[col_u], 0, 0, core_peer)

    def edge_pivot(number, there):
        return edge(rbuf.at[pivot_u], piv.at[1], 2 + number, 1, there)

    def edge_pivot_on():
        return edge(piv.at[1], piv.at[1], 2, 1, core_peer)

    def relay_copy():
        return pltpu.make_async_remote_copy(
            src_ref=rbuf.at[whole_u],
            dst_ref=relay,
            send_sem=xs.at[0],
            recv_sem=xr.at[0],
            device_id=(y_peer, front),
            device_id_type=MESH,
        )

    def relay_on():
        return pltpu.make_async_remote_copy(
            src_ref=relay,
            dst_ref=rbuf.at[col_u],
            send_sem=xs.at[0],
            recv_sem=er.at[0],
            device_id=(cube, 2),
            device_id_type=MESH,
        )

    relays = (front == 0) & (rho == 2)
    relays_on = (front == 0) & (rho == 3)

    def start_edges():
        @pl.when(rho == 0)
        def _():
            edge_pivot(0, core_peer).start()
            edge_pivot(1, y_peer).start()
            piv[1] = rbuf[pivot_u, :]

        @pl.when(holds_u)
        def _():
            edge_col(0, core_peer).start()

            @pl.when(front != 2)
            def _():
                edge_col(1, y_peer).start()

            rbuf[col_u, :] = rbuf[whole_u, :]

    @pl.when(front == 0)
    def _():
        def push(index, carry):
            chunk_copy(index, up).start()
            chunk_copy(index + HALF, down).start()
            return carry

        lax.fori_loop(0, HALF, push, 0)

        def push_core(index, carry):
            landed(index)
            return carry

        lax.fori_loop(0, 2 * HALF, push_core, 0)
        for half in range(2):
            upper_copy(half, 1, 2 * half).start()
            upper_copy(half, 3, 2 * half + 1).start()
        start_edges()

    @pl.when(relays)
    def _():
        relay_copy().start()

    own_rows = pl.ds(pl.multiple_of(pos_z * SLOTS, 8), SLOTS)
    r1[own_rows, :] = s1[own_rows, :]

    eye = iota((PIV, PIV), 0) == iota((PIV, PIV), 1)
    links = level[pl.ds(group, 1), :]
    two_rows = iota((16, 2048), 0)
    digits = jnp.where(two_rows == 0, links >> 4, jnp.where(two_rows == 1, links & 15, 0))
    digits = digits.astype(F32).astype(BF16)

    def prepare_leaf(leaf, carry):
        shift = signs[pl.ds(leaf, 1), :].astype(F32) * perturb[pl.ds(leaf, 1), :]
        leaf_inv[leaf] = newton_inverse(leaf_pivot[leaf] + jnp.where(eye, shift, 0.0))
        picked = mm(digits, hits(iota((2048, PIV), 0), leaf_map[pl.ds(leaf, 1), :]))
        composite = picked[0:1, :] * 16.0 + picked[1:2, :]
        kb[0, front, leaf, 128:136, :] = jnp.broadcast_to(composite, (8, PIV))
        return carry

    lax.fori_loop(0, 2, prepare_leaf, 0)

    @pl.when((front == 1) | (front == 2))
    def _():
        def forward(index, carry):
            chunk_copy(index, up).wait_recv()
            chunk_copy(index, up).start()
            landed(index)

            @pl.when(front == 2)
            def _():
                chunk_copy(index + HALF, down).wait_recv()
                chunk_copy(index + HALF, down).start()
                landed(index + HALF)

            return carry

        lax.fori_loop(0, HALF, forward, 0)

    @pl.when(front == 3)
    def _():
        def forward(index, carry):
            chunk_copy(index + HALF, down).wait_recv()
            chunk_copy(index + HALF, down).start()
            landed(index + HALF)
            return carry

        lax.fori_loop(0, HALF, forward, 0)

    def wait_z(step, carry):
        z_copy(step).wait_recv()
        return carry

    lax.fori_loop(1, depth_z, wait_z, 0)
    for place in range(PLANE):
        for slot in range(5):
            s2[place, slot] = r1[pl.ds(slot * PLANE + place, depth_z, stride=SLOTS), :]

    def d_copy(step):
        there = at_plane(step)
        return pltpu.make_async_remote_copy(
            src_ref=s2.at[there],
            dst_ref=r2.at[pos_d],
            send_sem=ds.at[step],
            recv_sem=dr.at[step],
            device_id=(plane_base + there, front),
            device_id_type=MESH,
        )

    def start_d(step, carry):
        d_copy(step).start()
        return carry

    lax.fori_loop(1, PLANE, start_d, 0)
    r2[pos_d] = s2[pos_d]

    @pl.when(relays_on)
    def _():
        relay_copy().wait_recv()
        relay_on().start()

    @pl.when((front == 1) | (front == 3))
    def _():
        def take(index, carry):
            number = index + (HALF // 2) * (3 - front)
            chunk_copy(number, up).wait_recv()
            landed(number)
            return carry

        lax.fori_loop(0, HALF, take, 0)

    def invert_set(number, carry):
        rows_two = piv[number, 128:256, 0:128]
        first = newton_inverse(piv[number, 0:128, 0:128])
        second = newton_inverse(
            piv[number, 128:256, 128:256] - exact(exact(rows_two, first), rows_two, NT)
        )
        inv_sets[number, 0] = first
        inv_sets[number, 1] = second
        inv_sets[number, 2] = rows_two
        return carry

    def wait_d(step, carry):
        d_copy(step).wait_recv()
        return carry

    lax.fori_loop(1, PLANE, wait_d, 0)

    slots_per = PLANE * depth_z
    marks_in = r2[:, 4].reshape(slots_per, PIV).T.astype(jnp.int32)
    arrivals = jnp.zeros((256, PIV), F32)
    for slot in range(4):
        to_row = hits(iota((256, slots_per), 0) + 1, marks_in[slot : slot + 1, :])
        got_high, got_low = halves(r2[:, slot].reshape(slots_per, PIV))
        arrivals = arrivals + mm(to_row, got_high) + mm(to_row, got_low)
    for leaf in range(2):
        coupling = leaf_coupling[leaf] + arrivals[leaf * PIV : (leaf + 1) * PIV, :]
        factor = exact(coupling, leaf_inv[leaf])
        factor_out[leaf] = factor
        kb[0, front, leaf, 0:128, :] = -exact(factor, coupling, NT)

    def k_copy(source, place, where, send, arrival, there):
        return pltpu.make_async_remote_copy(
            src_ref=kb.at[source, where],
            dst_ref=kb.at[place, where],
            send_sem=ks.at[send],
            recv_sem=kr.at[arrival],
            device_id=there,
            device_id_type=MESH,
        )

    def k_y():
        return k_copy(0, 2, front, 0, 0, (y_peer, front))

    def k_front(which, step):
        number = 1 + 3 * which + step - 1
        return k_copy(
            2 * which, 2 * which, front, number, number, (cube, (front + step) % 4)
        )

    def k_core(which, step):
        number = 7 + 4 * which + step
        return k_copy(
            2 * which,
            2 * which + 1,
            (front + 4 - step) % 4,
            number,
            number,
            (core_peer, front),
        )

    k_y().start()
    for step in (1, 3, 2):
        k_front(0, step).start()
    k_core(0, 0).start()

    @pl.when(low == 0)
    def _():
        piv[0] = rbuf[pivot_g, :]

    @pl.when(low != 0)
    def _():
        for part in range(8):
            pivot_copy(part).wait_recv()

    @pl.when(holds_g)
    def _():
        rbuf[col_g, :] = rbuf[first_g, :]

    lax.fori_loop(0, 1, invert_set, 0)

    def panel(index, carry):
        number = index // 3
        start = jnp.where(
            index < 2,
            low * 1024 + index * 512,
            jnp.where(index == 3, rho * 512, front * 512),
        )
        rows = pl.ds(pl.multiple_of(index * 512, 512), 512)
        place = iota((512, PIV), 0) + start
        first = rbuf[rows, 0:128]
        second = rbuf[rows, 128:256]
        past_one = place >= 128
        past_two = place >= 256
        lower_one = jnp.where(past_one, dot3(first, inv_sets[number, 0]), 0.0)
        second = second - dot3(lower_one, inv_sets[number, 2], NT)
        lower_two = jnp.where(past_two, dot3(second, inv_sets[number, 1]), 0.0)
        lfull[rows, 0:128] = lower_one
        lfull[rows, 128:256] = lower_two
        one_high, one_low = halves(lower_one)
        two_high, two_low = halves(lower_two)
        l_high[rows, 0:128] = one_high
        l_high[rows, 128:256] = two_high
        l_low[rows, 0:128] = one_low
        l_low[rows, 128:256] = two_low
        one_high, one_low = halves(jnp.where(past_one, first, 0.0))
        two_high, two_low = halves(jnp.where(past_two, second, 0.0))
        p_high[rows, 0:128] = one_high
        p_high[rows, 128:256] = two_high
        p_low[rows, 0:128] = one_low
        p_low[rows, 128:256] = two_low
        return carry

    lax.fori_loop(0, 2, panel, 0)

    @pl.when(low != front // 2)
    def _():
        for part in range(HALF):
            col_copy(part).wait_recv()

    lax.fori_loop(2, 3, panel, 0)

    def update(l_rows, p_rows):
        return mm(l_high[l_rows, :], p_high[p_rows, :], NT) + (
            mm(l_high[l_rows, :], p_low[p_rows, :], NT)
            + mm(l_low[l_rows, :], p_high[p_rows, :], NT)
        )

    def quarter_map(quarter):
        entries = level[pl.ds(group, 1), pl.ds(pl.multiple_of(quarter * 512, 512), 512)]
        kept = iota((1, 512), 1) + quarter * 512 >= 256
        return hits(iota((512, 512), 0), jnp.where(kept, entries - quarter * 512, -1))

    col_hits = quarter_map(front)

    def link(turn, carry):
        half = turn * high + (1 - turn) * (1 - high)
        rows = pl.ds(pl.multiple_of(half * 512, 512), 512)
        schur = mid[rows, :].astype(F32) - update(rows, col_g)
        s_high, s_low = halves(schur)
        t_high, t_low = halves(mm(s_high, col_hits, NT) + mm(s_low, col_hits, NT))
        row_hits = quarter_map(2 * low + half)
        vout[turn] = mm(row_hits, t_high) + mm(row_hits, t_low)
        return carry

    def v_copy(half):
        rows = pl.ds(256 * half, 256)
        return pltpu.make_async_remote_copy(
            src_ref=vout.at[0, rows],
            dst_ref=vin.at[rows],
            send_sem=vs.at[half],
            recv_sem=vr.at[half],
            device_id=(y_peer, front),
            device_id_type=MESH,
        )

    lax.fori_loop(0, 1, link, 0)
    @pl.when(rho != 1)
    def _():
        v_copy(0).start()

    v_copy(1).start()
    @pl.when((front == 1) | (front == 3))
    def _():
        half_one = pl.ds(pl.multiple_of(1536 + 128 * (front - 1), 256), 256)
        passed = pltpu.make_async_remote_copy(
            src_ref=rbuf.at[half_one],
            dst_ref=rbuf.at[half_one],
            send_sem=us.at[0],
            recv_sem=ur.at[(front - 1) // 2],
            device_id=(cube, 2),
            device_id_type=MESH,
        )
        passed.wait_recv()
        passed.start()

    @pl.when((front == 1) | (front == 3))
    def _():
        upper_copy(1 - (front - 1) // 2, 1, 0).wait_recv()
        start_edges()


    mid_factor_out[...] = lfull[pl.ds(pl.multiple_of(front * 256, 256), 256), :]

    k_y().wait_recv()
    for step in (1, 3, 2):
        k_front(1, step).start()
    k_core(1, 0).start()
    lax.fori_loop(1, 2, link, 0)
    upper_out[...] = top[...].astype(F32) + vout[1]

    @pl.when(front == 2)
    def _():
        upper_copy(0, 1, 0).wait_recv()
        upper_copy(1, 1, 0).wait_recv()
        start_edges()

    ids = iota((512, PIV), 0)

    def gather_group(which, carry):
        def one(index, inner):
            entry = index // 2
            leaf = index % 2
            composite = kb[which, entry, leaf, 128:129, :].astype(jnp.int32)
            cols = pl.ds(pl.multiple_of(index * PIV, PIV), PIV)
            rt[:, cols] = hits(ids, composite - rho * 512)
            col_ids = hits(ids, composite - front * 512)
            k_high, k_low = halves(kb[which, entry, leaf, 0:128, :])
            spread_high, spread_low = halves(mm(k_high, col_ids, NT) + mm(k_low, col_ids, NT))
            kr_high[cols, :] = spread_high
            kr_low[cols, :] = spread_low
            return inner

        lax.fori_loop(0, 8, one, 0, unroll=True)
        upper_out[...] += mm(rt[...], kr_high[...]) + mm(rt[...], kr_low[...])
        return carry

    for step in (1, 3, 2):
        k_front(0, step).wait_recv()
        k_core(0, step).start()
        k_front(1, step).wait_recv()
        k_core(1, step).start()

    lax.fori_loop(0, 2, lambda turn, carry: gather_group(2 * turn, carry), 0)

    rho_y = rho + 1 - 2 * high

    @pl.when(rho_y == 0)
    def _():
        edge_pivot(0, core_peer).wait_recv()
        edge_pivot_on().start()

    @pl.when(rho_y == front)
    def _():
        edge_col(0, core_peer).wait_recv()
        edge_col_on().start()

    for step in range(4):
        k_core(0, step).wait_recv()
        k_core(1, step).wait_recv()
    lax.fori_loop(0, 2, lambda turn, carry: gather_group(2 * turn + 1, carry), 0)

    @pl.when((rho != 0) & (rho_y != 0))
    def _():
        edge_pivot(0, core_peer).wait_recv()

    lax.fori_loop(1, 2, invert_set, 0)
    lax.fori_loop(3, 4, panel, 0)

    @pl.when((rho != front) & (rho_y != front))
    def _():
        edge_col(0, core_peer).wait_recv()

    lax.fori_loop(4, 5, panel, 0)
    upper_out[...] += -update(whole_u, col_u)
    v_copy(1).wait_recv()
    upper_out[256:512, :] += vin[256:512, :]

    @pl.when(rho != 0)
    def _():
        v_copy(0).wait_recv()
        upper_out[0:256, :] += vin[0:256, :]

    def end_z(step, carry):
        z_copy(step).wait_send()
        return carry

    def end_d(step, carry):
        d_copy(step).wait_send()
        return carry

    lax.fori_loop(1, depth_z, end_z, 0)
    lax.fori_loop(1, PLANE, end_d, 0)

    @pl.when(front != 3)
    def _():
        def end_up(index, carry):
            chunk_copy(index, up).wait_send()
            return carry

        lax.fori_loop(0, HALF, end_up, 0)

    @pl.when(front != 1)
    def _():
        def end_down(index, carry):
            chunk_copy(index, down).wait_send()
            return carry

        lax.fori_loop(HALF, 2 * HALF, end_down, 0)

    @pl.when(low == 0)
    def _():
        for part in range(8):
            pivot_copy(part).wait_send()

    @pl.when(holds_g)
    def _():
        for part in range(HALF):
            col_copy(part).wait_send()

    @pl.when(front == 0)
    def _():
        for number in range(4):
            upper_copy(0, 1, number).wait_send()

    @pl.when((front == 1) | (front == 3))
    def _():
        upper_copy(0, 2, 0).wait_send()

    @pl.when(rho == 0)
    def _():
        edge_pivot(0, core_peer).wait_send()
        edge_pivot(1, y_peer).wait_send()

    @pl.when(rho_y == 0)
    def _():
        edge_pivot_on().wait_send()

    @pl.when(holds_u)
    def _():
        edge_col(0, core_peer).wait_send()

        @pl.when(front != 2)
        def _():
            edge_col(1, y_peer).wait_send()

    @pl.when(relays)
    def _():
        relay_copy().wait_send()

    @pl.when(relays_on)
    def _():
        relay_on().wait_send()

    @pl.when(rho_y == front)
    def _():
        edge_col_on().wait_send()

    v_copy(1).wait_send()

    @pl.when(rho != 1)
    def _():
        v_copy(0).wait_send()
    k_y().wait_send()
    for which in range(2):
        for step in range(1, 4):
            k_front(which, step).wait_send()
        for step in range(4):
            k_core(which, step).wait_send()


def hand_out(factor_in, mid_factor_in, upper_in, factor_out, mid_factor_out, upper_out):
    factor_out[...] = factor_in[...]
    mid_factor_out[...] = mid_factor_in[...]
    upper_out[...] = upper_in[...]


def local(
    kkt_blocks,
    kkt_owner,
    kkt_target,
    leaf_pivot,
    pivot_signs,
    perturb,
    leaf_coupling,
    leaf_map,
    mid_front,
    level_map,
    top_front,
):
    depth_z = lax.axis_size("cube") // PLANE
    vmem = pl.BlockSpec(memory_space=pltpu.VMEM)
    dma = pltpu.SemaphoreType.DMA
    results = (
        jax.ShapeDtypeStruct((2, PIV, PIV), F32),
        jax.ShapeDtypeStruct((256, 256), F32),
        jax.ShapeDtypeStruct((512, 512), F32),
    )
    computed = pl.pallas_call(
        functools.partial(fused, depth_z),
        out_shape=results,
        in_specs=[vmem] * 11,
        out_specs=(vmem, vmem, vmem),
        scratch_shapes=[
            pltpu.VMEM((depth_z * SLOTS, PIV), F32),
            pltpu.VMEM((depth_z * SLOTS, PIV), F32),
            pltpu.VMEM((PLANE, 5, depth_z, PIV), F32),
            pltpu.VMEM((PLANE, 5, depth_z, PIV), F32),
            pltpu.VMEM((2560, 256), F32),
            pltpu.VMEM((512, 256), F32),
            pltpu.VMEM((2, 256, 256), F32),
            pltpu.VMEM((2, 3, PIV, PIV), F32),
            pltpu.VMEM((2, PIV, PIV), F32),
            pltpu.VMEM((2560, 256), F32),
            pltpu.VMEM((2560, 256), BF16),
            pltpu.VMEM((2560, 256), BF16),
            pltpu.VMEM((2560, 256), BF16),
            pltpu.VMEM((2560, 256), BF16),
            pltpu.VMEM((2, 512, 512), F32),
            pltpu.VMEM((512, 512), F32),
            pltpu.VMEM((4, 4, 2, 136, PIV), F32),
            pltpu.VMEM((512, 1024), BF16),
            pltpu.VMEM((1024, 512), BF16),
            pltpu.VMEM((1024, 512), BF16),
            dma((depth_z,)),
            dma((depth_z,)),
            dma((PLANE,)),
            dma((PLANE,)),
            dma((2 * HALF,)),
            dma((2 * HALF,)),
            dma((HALF,)),
            dma((HALF,)),
            dma((8,)),
            dma((8,)),
            dma((4,)),
            dma((2,)),
            dma((4,)),
            dma((2,)),
            dma((1,)),
            dma((1,)),
            dma((2,)),
            dma((2,)),
            dma((15,)),
            dma((15,)),
        ],
        compiler_params=pltpu.CompilerParams(
            collective_id=0, has_side_effects=True, vmem_limit_bytes=56 * 1024 * 1024
        ),
    )(
        kkt_blocks,
        kkt_owner.reshape(1, -1),
        kkt_target,
        leaf_pivot,
        pivot_signs,
        perturb,
        leaf_coupling,
        leaf_map,
        mid_front,
        level_map,
        top_front,
    )
    return pl.pallas_call(
        hand_out,
        out_shape=results,
        in_specs=[vmem] * 3,
        out_specs=(vmem,) * 3,
    )(*computed)


def solution(mesh):
    in_specs = (
        P("front", "cube", None),
        P("front", "cube", None),
        P("front", "cube"),
        P("cube", "front", None),
        P("cube", "front"),
        P("cube", "front"),
        P("cube", "front", None),
        P("cube", "front"),
        P("cube", "front"),
        P(),
        P("cube", "front"),
    )
    out_specs = (P("cube", "front", None), P(("cube", "front"), None), P("cube", "front"))
    return jax.shard_map(local, mesh=mesh, in_specs=in_specs, out_specs=out_specs, check_vma=False)
```

```python
import functools

import jax
import jax.numpy as jnp
from jax import lax
from jax.experimental import pallas as pl
from jax.experimental.pallas import tpu as pltpu
from jax.sharding import PartitionSpec as P

PIV = 128
QUARTER = 512
PLANE = 8
SLOTS = 40
CHUNK = 32
HALF = 16
F32 = jnp.float32
BF16 = jnp.bfloat16
MESH = pl.DeviceIdType.MESH
NN = (((1,), (0,)), ((), ()))
NT = (((1,), (1,)), ((), ()))


def mm(a, b, dims=NN):
    return lax.dot_general(a, b, dims, preferred_element_type=F32)


def exact(a, b, dims=NN):
    return lax.dot_general(
        a, b, dims, precision=lax.Precision.HIGHEST, preferred_element_type=F32
    )


def halves(a):
    high = a.astype(BF16)
    return high, (a - high.astype(F32)).astype(BF16)


def dot3(a, b, dims=NN):
    a_high, a_low = halves(a)
    b_high, b_low = halves(b)
    return mm(a_high, b_high, dims) + (mm(a_high, b_low, dims) + mm(a_low, b_high, dims))


def iota(shape, axis):
    return lax.broadcasted_iota(jnp.int32, shape, axis)


def hits(a, b):
    return jnp.where(a == b, 1.0, 0.0).astype(BF16)


def newton_inverse(block):
    eye = iota((PIV, PIV), 0) == iota((PIV, PIV), 1)
    on_diagonal = jnp.where(eye, block, 0.0)
    by_col = 1.0 / jnp.sum(on_diagonal, axis=0, keepdims=True)
    by_row = 1.0 / jnp.sum(on_diagonal, axis=1, keepdims=True)
    current = jnp.where(eye, 2.0 * by_col, 0.0) - by_row * (block * by_col)
    return 2.0 * current - exact(current, exact(block, current))


def fused(
    depth_z,
    blocks,
    owner,
    target,
    leaf_pivot,
    signs,
    perturb,
    leaf_coupling,
    leaf_map,
    mid,
    level,
    top,
    factor_out,
    mid_factor_out,
    upper_out,
    s1,
    r1,
    s2,
    r2,
    rbuf,
    relay,
    piv,
    inv_sets,
    leaf_inv,
    lfull,
    l_high,
    l_low,
    p_high,
    p_low,
    vout,
    vin,
    kb,
    rt,
    kr_high,
    kr_low,
    zs,
    zr,
    ds,
    dr,
    ps,
    pr,
    gs,
    gr,
    hs,
    hr,
    us,
    ur,
    es,
    er,
    xs,
    xr,
    ts,
    vs,
    vr,
    ks,
    kr,
):
    cube = lax.axis_index("cube")
    front = lax.axis_index("front")
    pos_z = cube // PLANE
    pos_d = cube % PLANE
    low = cube % 2
    high = (cube // 2) % 2
    rho = 2 * low + high
    core_peer = cube + 1 - 2 * low
    y_peer = cube + 2 - 4 * high
    plane_base = cube - pos_d
    group = cube // 2
    row_count = blocks.shape[1]
    cube_count = depth_z * PLANE

    def at_z(step):
        return (pos_z + step) % depth_z

    def at_plane(step):
        return (pos_d + step) % PLANE

    barrier = pltpu.get_barrier_semaphore()

    def greet_z(step, carry):
        pl.semaphore_signal(
            barrier, inc=1, device_id=(at_z(step) * PLANE + pos_d, front), device_id_type=MESH
        )
        return carry

    def greet_plane(step, carry):
        pl.semaphore_signal(
            barrier, inc=1, device_id=(plane_base + at_plane(step), front), device_id_type=MESH
        )
        return carry

    lax.fori_loop(1, depth_z, greet_z, 0)
    lax.fori_loop(1, PLANE, greet_plane, 0)
    for step in range(1, 4):
        pl.semaphore_signal(
            barrier, inc=1, device_id=(cube, (front + step) % 4), device_id_type=MESH
        )

    @pl.when(front == 0)
    def _():
        rbuf[0:1024, :] = mid[:, 0:256].astype(F32)
        rbuf[1536:2048, :] = top[:, 0:256].astype(F32)

    own = owner[...]
    own_mask = iota((cube_count, row_count), 0) == own
    own_hits = jnp.where(own_mask, 1.0, 0.0).astype(BF16)
    before = jnp.where(
        iota((row_count, row_count), 0) < iota((row_count, row_count), 1), 1.0, 0.0
    ).astype(BF16)
    ahead = mm(own_hits, before)
    rank = jnp.sum(jnp.where(own_mask, ahead, 0.0), axis=0, keepdims=True).astype(jnp.int32)
    base = (own >> 3) * SLOTS + (own & 7)
    send_rows = depth_z * SLOTS
    row_ids = iota((send_rows, row_count), 0)
    to_slot = hits(row_ids, base + rank * PLANE)
    value_high, value_low = halves(blocks[0])
    marks = jnp.where(row_ids == base + 32, (target[...] + 1).astype(F32), 0.0).astype(BF16)
    by_rank = hits(iota((PIV, row_count), 0), rank)
    s1[...] = mm(to_slot, value_high) + mm(to_slot, value_low) + mm(marks, by_rank, NT)

    pl.semaphore_wait(barrier, depth_z + PLANE + 1)

    def z_copy(step):
        there = at_z(step)
        return pltpu.make_async_remote_copy(
            src_ref=s1.at[pl.ds(pl.multiple_of(there * SLOTS, 8), SLOTS)],
            dst_ref=r1.at[pl.ds(pl.multiple_of(pos_z * SLOTS, 8), SLOTS)],
            send_sem=zs.at[step],
            recv_sem=zr.at[step],
            device_id=(there * PLANE + pos_d, front),
            device_id_type=MESH,
        )

    def start_z(step, carry):
        z_copy(step).start()
        return carry

    lax.fori_loop(1, depth_z, start_z, 0)

    def chunk_copy(index, there):
        rows = pl.ds(pl.multiple_of(index * CHUNK, CHUNK), CHUNK)
        return pltpu.make_async_remote_copy(
            src_ref=rbuf.at[rows],
            dst_ref=rbuf.at[rows],
            send_sem=ps.at[index],
            recv_sem=pr.at[index],
            device_id=(cube, there),
            device_id_type=MESH,
        )

    up = (front + 1) % 4
    down = (front + 3) % 4
    holds_g = low == front // 2
    holds_u = rho == front
    col_g = pl.ds(1024, 512)
    col_u = pl.ds(2048, 512)
    first_g = pl.ds(pl.multiple_of((front % 2) * 512, 512), 512)
    pivot_g = pl.ds(0, 256)
    pivot_u = pl.ds(1536, 256)
    whole_u = pl.ds(1536, 512)

    def col_copy(part):
        start = (front % 2) * 512 + part * CHUNK
        return pltpu.make_async_remote_copy(
            src_ref=rbuf.at[pl.ds(pl.multiple_of(start, CHUNK), CHUNK)],
            dst_ref=rbuf.at[pl.ds(pl.multiple_of(1024 + part * CHUNK, CHUNK), CHUNK)],
            send_sem=gs.at[part],
            recv_sem=gr.at[part],
            device_id=(core_peer, front),
            device_id_type=MESH,
        )

    def pivot_copy(part):
        rows = pl.ds(pl.multiple_of(part * CHUNK, CHUNK), CHUNK)
        return pltpu.make_async_remote_copy(
            src_ref=rbuf.at[rows],
            dst_ref=piv.at[0, rows],
            send_sem=hs.at[part],
            recv_sem=hr.at[part],
            device_id=(core_peer, front),
            device_id_type=MESH,
        )

    def landed(index):
        @pl.when((low == 0) & (index < 8))
        def _():
            pivot_copy(index).start()

        @pl.when(holds_g & (index // HALF == front % 2))
        def _():
            col_copy(index % HALF).start()

    def upper_copy(half, there, number):
        rows = pl.ds(pl.multiple_of(1536 + 256 * half, 256), 256)
        return pltpu.make_async_remote_copy(
            src_ref=rbuf.at[rows],
            dst_ref=rbuf.at[rows],
            send_sem=us.at[number],
            recv_sem=ur.at[half],
            device_id=(cube, there),
            device_id_type=MESH,
        )

    def edge(source, place, number, arrival, there):
        return pltpu.make_async_remote_copy(
            src_ref=source,
            dst_ref=place,
            send_sem=es.at[number],
            recv_sem=er.at[arrival],
            device_id=(there, front),
            device_id_type=MESH,
        )

    def edge_col(number, there):
        return edge(rbuf.at[whole_u], rbuf.at[col_u], number, 0, there)

    def edge_col_on():
        return edge(rbuf.at[col_u], rbuf.at[col_u], 0, 0, core_peer)

    def edge_pivot(number, there):
        return edge(rbuf.at[pivot_u], piv.at[1], 2 + number, 1, there)

    def edge_pivot_on():
        return edge(piv.at[1], piv.at[1], 2, 1, core_peer)

    rho_y = rho + 1 - 2 * high

    def relay_copy():
        return pltpu.make_async_remote_copy(
            src_ref=rbuf.at[whole_u],
            dst_ref=relay,
            send_sem=xs.at[0],
            recv_sem=xr.at[0],
            device_id=(y_peer, front),
            device_id_type=MESH,
        )

    def relay_on():
        return pltpu.make_async_remote_copy(
            src_ref=relay,
            dst_ref=rbuf.at[col_u],
            send_sem=xs.at[0],
            recv_sem=er.at[0],
            device_id=(cube, rho_y),
            device_id_type=MESH,
        )

    def pivot_on(there):
        return pltpu.make_async_remote_copy(
            src_ref=piv.at[1],
            dst_ref=piv.at[1],
            send_sem=ts.at[there],
            recv_sem=er.at[1],
            device_id=(cube, there),
            device_id_type=MESH,
        )

    relays = (front == 0) & (rho != 0)
    relays_on = (front == 0) & (rho_y != 0)
    pivots_on = (front == 0) & (rho_y == 0)

    def start_edges():
        @pl.when(rho == 0)
        def _():
            edge_pivot(0, core_peer).start()

            @pl.when(front == 0)
            def _():
                edge_pivot(1, y_peer).start()

            piv[1] = rbuf[pivot_u, :]

        @pl.when(holds_u)
        def _():
            edge_col(0, core_peer).start()

            @pl.when(front == 0)
            def _():
                edge_col(1, y_peer).start()

            rbuf[col_u, :] = rbuf[whole_u, :]

    @pl.when(front == 0)
    def _():
        def push(index, carry):
            chunk_copy(index, up).start()
            chunk_copy(index + HALF, down).start()
            return carry

        lax.fori_loop(0, HALF, push, 0)

        def push_core(index, carry):
            landed(index)
            return carry

        lax.fori_loop(0, 2 * HALF, push_core, 0)
        for half in range(2):
            upper_copy(half, 1, 2 * half).start()
            upper_copy(half, 3, 2 * half + 1).start()
        start_edges()

    @pl.when(relays)
    def _():
        relay_copy().start()

    @pl.when(pivots_on)
    def _():
        edge_pivot(0, core_peer).wait_recv()
        edge_pivot_on().start()
        for there in (2, 1, 3):
            pivot_on(there).start()

    own_rows = pl.ds(pl.multiple_of(pos_z * SLOTS, 8), SLOTS)
    r1[own_rows, :] = s1[own_rows, :]

    eye = iota((PIV, PIV), 0) == iota((PIV, PIV), 1)
    links = level[pl.ds(group, 1), :]
    two_rows = iota((16, 2048), 0)
    digits = jnp.where(two_rows == 0, links >> 4, jnp.where(two_rows == 1, links & 15, 0))
    digits = digits.astype(F32).astype(BF16)

    def prepare_leaf(leaf, carry):
        shift = signs[pl.ds(leaf, 1), :].astype(F32) * perturb[pl.ds(leaf, 1), :]
        leaf_inv[leaf] = newton_inverse(leaf_pivot[leaf] + jnp.where(eye, shift, 0.0))
        picked = mm(digits, hits(iota((2048, PIV), 0), leaf_map[pl.ds(leaf, 1), :]))
        composite = picked[0:1, :] * 16.0 + picked[1:2, :]
        kb[0, front, leaf, 128:136, :] = jnp.broadcast_to(composite, (8, PIV))
        return carry

    lax.fori_loop(0, 2, prepare_leaf, 0)

    @pl.when((front == 1) | (front == 2))
    def _():
        def forward(index, carry):
            chunk_copy(index, up).wait_recv()
            chunk_copy(index, up).start()
            landed(index)

            @pl.when(front == 2)
            def _():
                chunk_copy(index + HALF, down).wait_recv()
                chunk_copy(index + HALF, down).start()
                landed(index + HALF)

            return carry

        lax.fori_loop(0, HALF, forward, 0)

    @pl.when(front == 3)
    def _():
        def forward(index, carry):
            chunk_copy(index + HALF, down).wait_recv()
            chunk_copy(index + HALF, down).start()
            landed(index + HALF)
            return carry

        lax.fori_loop(0, HALF, forward, 0)

    def wait_z(step, carry):
        z_copy(step).wait_recv()
        return carry

    lax.fori_loop(1, depth_z, wait_z, 0)
    for place in range(PLANE):
        for slot in range(5):
            s2[place, slot] = r1[pl.ds(slot * PLANE + place, depth_z, stride=SLOTS), :]

    def d_copy(step):
        there = at_plane(step)
        return pltpu.make_async_remote_copy(
            src_ref=s2.at[there],
            dst_ref=r2.at[pos_d],
            send_sem=ds.at[step],
            recv_sem=dr.at[step],
            device_id=(plane_base + there, front),
            device_id_type=MESH,
        )

    def start_d(step, carry):
        d_copy(step).start()
        return carry

    lax.fori_loop(1, PLANE, start_d, 0)
    r2[pos_d] = s2[pos_d]

    @pl.when(relays_on)
    def _():
        relay_copy().wait_recv()
        relay_on().start()

    @pl.when((front == 1) | (front == 3))
    def _():
        def take(index, carry):
            number = index + (HALF // 2) * (3 - front)
            chunk_copy(number, up).wait_recv()
            landed(number)
            return carry

        lax.fori_loop(0, HALF, take, 0)

    def invert_set(number, carry):
        rows_two = piv[number, 128:256, 0:128]
        first = newton_inverse(piv[number, 0:128, 0:128])
        second = newton_inverse(
            piv[number, 128:256, 128:256] - exact(exact(rows_two, first), rows_two, NT)
        )
        inv_sets[number, 0] = first
        inv_sets[number, 1] = second
        inv_sets[number, 2] = rows_two
        return carry

    def wait_d(step, carry):
        d_copy(step).wait_recv()
        return carry

    lax.fori_loop(1, PLANE, wait_d, 0)

    slots_per = PLANE * depth_z
    marks_in = r2[:, 4].reshape(slots_per, PIV).T.astype(jnp.int32)
    arrivals = jnp.zeros((256, PIV), F32)
    for slot in range(4):
        to_row = hits(iota((256, slots_per), 0) + 1, marks_in[slot : slot + 1, :])
        got_high, got_low = halves(r2[:, slot].reshape(slots_per, PIV))
        arrivals = arrivals + mm(to_row, got_high) + mm(to_row, got_low)
    for leaf in range(2):
        coupling = leaf_coupling[leaf] + arrivals[leaf * PIV : (leaf + 1) * PIV, :]
        factor = exact(coupling, leaf_inv[leaf])
        factor_out[leaf] = factor
        kb[0, front, leaf, 0:128, :] = -exact(factor, coupling, NT)

    def k_copy(source, place, where, send, arrival, there):
        return pltpu.make_async_remote_copy(
            src_ref=kb.at[source, where],
            dst_ref=kb.at[place, where],
            send_sem=ks.at[send],
            recv_sem=kr.at[arrival],
            device_id=there,
            device_id_type=MESH,
        )

    def k_y():
        return k_copy(0, 2, front, 0, 0, (y_peer, front))

    def k_front(which, step):
        number = 1 + 3 * which + step - 1
        return k_copy(
            2 * which, 2 * which, front, number, number, (cube, (front + step) % 4)
        )

    def k_core(which, step):
        number = 7 + 4 * which + step
        return k_copy(
            2 * which,
            2 * which + 1,
            (front + 4 - step) % 4,
            number,
            number,
            (core_peer, front),
        )

    k_y().start()
    for step in (1, 3, 2):
        k_front(0, step).start()
    k_core(0, 0).start()

    @pl.when(low == 0)
    def _():
        piv[0] = rbuf[pivot_g, :]

    @pl.when(low != 0)
    def _():
        for part in range(8):
            pivot_copy(part).wait_recv()

    @pl.when(holds_g)
    def _():
        rbuf[col_g, :] = rbuf[first_g, :]

    lax.fori_loop(0, 1, invert_set, 0)

    def panel(index, carry):
        number = index // 3
        start = jnp.where(
            index < 2,
            low * 1024 + index * 512,
            jnp.where(index == 3, rho * 512, front * 512),
        )
        rows = pl.ds(pl.multiple_of(index * 512, 512), 512)
        place = iota((512, PIV), 0) + start
        first = rbuf[rows, 0:128]
        second = rbuf[rows, 128:256]
        past_one = place >= 128
        past_two = place >= 256
        lower_one = jnp.where(past_one, dot3(first, inv_sets[number, 0]), 0.0)
        second = second - dot3(lower_one, inv_sets[number, 2], NT)
        lower_two = jnp.where(past_two, dot3(second, inv_sets[number, 1]), 0.0)
        lfull[rows, 0:128] = lower_one
        lfull[rows, 128:256] = lower_two
        one_high, one_low = halves(lower_one)
        two_high, two_low = halves(lower_two)
        l_high[rows, 0:128] = one_high
        l_high[rows, 128:256] = two_high
        l_low[rows, 0:128] = one_low
        l_low[rows, 128:256] = two_low
        one_high, one_low = halves(jnp.where(past_one, first, 0.0))
        two_high, two_low = halves(jnp.where(past_two, second, 0.0))
        p_high[rows, 0:128] = one_high
        p_high[rows, 128:256] = two_high
        p_low[rows, 0:128] = one_low
        p_low[rows, 128:256] = two_low
        return carry

    lax.fori_loop(0, 2, panel, 0)

    @pl.when(low != front // 2)
    def _():
        for part in range(HALF):
            col_copy(part).wait_recv()

    lax.fori_loop(2, 3, panel, 0)

    def update(l_rows, p_rows):
        return mm(l_high[l_rows, :], p_high[p_rows, :], NT) + (
            mm(l_high[l_rows, :], p_low[p_rows, :], NT)
            + mm(l_low[l_rows, :], p_high[p_rows, :], NT)
        )

    def quarter_map(quarter):
        entries = level[pl.ds(group, 1), pl.ds(pl.multiple_of(quarter * 512, 512), 512)]
        kept = iota((1, 512), 1) + quarter * 512 >= 256
        return hits(iota((512, 512), 0), jnp.where(kept, entries - quarter * 512, -1))

    col_hits = quarter_map(front)

    def link(turn, carry):
        half = turn * high + (1 - turn) * (1 - high)
        rows = pl.ds(pl.multiple_of(half * 512, 512), 512)
        schur = mid[rows, :].astype(F32) - update(rows, col_g)
        s_high, s_low = halves(schur)
        t_high, t_low = halves(mm(s_high, col_hits, NT) + mm(s_low, col_hits, NT))
        row_hits = quarter_map(2 * low + half)
        vout[turn] = mm(row_hits, t_high) + mm(row_hits, t_low)
        return carry

    def v_copy(half):
        rows = pl.ds(256 * half, 256)
        return pltpu.make_async_remote_copy(
            src_ref=vout.at[0, rows],
            dst_ref=vin.at[rows],
            send_sem=vs.at[half],
            recv_sem=vr.at[half],
            device_id=(y_peer, front),
            device_id_type=MESH,
        )

    lax.fori_loop(0, 1, link, 0)
    @pl.when(rho != 1)
    def _():
        v_copy(0).start()

    v_copy(1).start()
    @pl.when((front == 1) | (front == 3))
    def _():
        half_one = pl.ds(pl.multiple_of(1536 + 128 * (front - 1), 256), 256)
        passed = pltpu.make_async_remote_copy(
            src_ref=rbuf.at[half_one],
            dst_ref=rbuf.at[half_one],
            send_sem=us.at[0],
            recv_sem=ur.at[(front - 1) // 2],
            device_id=(cube, 2),
            device_id_type=MESH,
        )
        passed.wait_recv()
        passed.start()

    @pl.when((front == 1) | (front == 3))
    def _():
        upper_copy(1 - (front - 1) // 2, 1, 0).wait_recv()
        start_edges()


    mid_factor_out[...] = lfull[pl.ds(pl.multiple_of(front * 256, 256), 256), :]

    k_y().wait_recv()
    for step in (1, 3, 2):
        k_front(1, step).start()
    k_core(1, 0).start()
    lax.fori_loop(1, 2, link, 0)
    upper_out[...] = top[...].astype(F32) + vout[1]

    @pl.when(front == 2)
    def _():
        upper_copy(0, 1, 0).wait_recv()
        upper_copy(1, 1, 0).wait_recv()
        start_edges()

    ids = iota((512, PIV), 0)

    def gather_group(which, carry):
        def one(index, inner):
            entry = index // 2
            leaf = index % 2
            composite = kb[which, entry, leaf, 128:129, :].astype(jnp.int32)
            cols = pl.ds(pl.multiple_of(index * PIV, PIV), PIV)
            rt[:, cols] = hits(ids, composite - rho * 512)
            col_ids = hits(ids, composite - front * 512)
            k_high, k_low = halves(kb[which, entry, leaf, 0:128, :])
            spread_high, spread_low = halves(mm(k_high, col_ids, NT) + mm(k_low, col_ids, NT))
            kr_high[cols, :] = spread_high
            kr_low[cols, :] = spread_low
            return inner

        lax.fori_loop(0, 8, one, 0, unroll=True)
        upper_out[...] += mm(rt[...], kr_high[...]) + mm(rt[...], kr_low[...])
        return carry

    for step in (1, 3, 2):
        k_front(0, step).wait_recv()
        k_core(0, step).start()
        k_front(1, step).wait_recv()
        k_core(1, step).start()

    lax.fori_loop(0, 2, lambda turn, carry: gather_group(2 * turn, carry), 0)

    @pl.when((rho_y == 0) & (front != 0))
    def _():
        edge_pivot(0, core_peer).wait_recv()
        edge_pivot_on().start()

    @pl.when(rho_y == front)
    def _():
        edge_col(0, core_peer).wait_recv()
        edge_col_on().start()

    for step in range(4):
        k_core(0, step).wait_recv()
        k_core(1, step).wait_recv()
    lax.fori_loop(0, 2, lambda turn, carry: gather_group(2 * turn + 1, carry), 0)

    @pl.when((rho != 0) & (rho_y != 0))
    def _():
        edge_pivot(0, core_peer).wait_recv()

    lax.fori_loop(1, 2, invert_set, 0)
    lax.fori_loop(3, 4, panel, 0)

    @pl.when((rho != front) & (rho_y != front))
    def _():
        edge_col(0, core_peer).wait_recv()

    lax.fori_loop(4, 5, panel, 0)
    upper_out[...] += -update(whole_u, col_u)
    v_copy(1).wait_recv()
    upper_out[256:512, :] += vin[256:512, :]

    @pl.when(rho != 0)
    def _():
        v_copy(0).wait_recv()
        upper_out[0:256, :] += vin[0:256, :]

    def end_z(step, carry):
        z_copy(step).wait_send()
        return carry

    def end_d(step, carry):
        d_copy(step).wait_send()
        return carry

    lax.fori_loop(1, depth_z, end_z, 0)
    lax.fori_loop(1, PLANE, end_d, 0)

    @pl.when(front != 3)
    def _():
        def end_up(index, carry):
            chunk_copy(index, up).wait_send()
            return carry

        lax.fori_loop(0, HALF, end_up, 0)

    @pl.when(front != 1)
    def _():
        def end_down(index, carry):
            chunk_copy(index, down).wait_send()
            return carry

        lax.fori_loop(HALF, 2 * HALF, end_down, 0)

    @pl.when(low == 0)
    def _():
        for part in range(8):
            pivot_copy(part).wait_send()

    @pl.when(holds_g)
    def _():
        for part in range(HALF):
            col_copy(part).wait_send()

    @pl.when(front == 0)
    def _():
        for number in range(4):
            upper_copy(0, 1, number).wait_send()

    @pl.when((front == 1) | (front == 3))
    def _():
        upper_copy(0, 2, 0).wait_send()

    @pl.when(rho == 0)
    def _():
        edge_pivot(0, core_peer).wait_send()

        @pl.when(front == 0)
        def _():
            edge_pivot(1, y_peer).wait_send()

    @pl.when(rho_y == 0)
    def _():
        edge_pivot_on().wait_send()

    @pl.when(holds_u)
    def _():
        edge_col(0, core_peer).wait_send()

        @pl.when(front == 0)
        def _():
            edge_col(1, y_peer).wait_send()

    @pl.when(relays)
    def _():
        relay_copy().wait_send()

    @pl.when(relays_on)
    def _():
        relay_on().wait_send()

    @pl.when(pivots_on)
    def _():
        for there in (1, 2, 3):
            pivot_on(there).wait_send()

    @pl.when(rho_y == front)
    def _():
        edge_col_on().wait_send()

    v_copy(1).wait_send()

    @pl.when(rho != 1)
    def _():
        v_copy(0).wait_send()
    k_y().wait_send()
    for which in range(2):
        for step in range(1, 4):
            k_front(which, step).wait_send()
        for step in range(4):
            k_core(which, step).wait_send()


def hand_out(factor_in, mid_factor_in, upper_in, factor_out, mid_factor_out, upper_out):
    factor_out[...] = factor_in[...]
    mid_factor_out[...] = mid_factor_in[...]
    upper_out[...] = upper_in[...]


def local(
    kkt_blocks,
    kkt_owner,
    kkt_target,
    leaf_pivot,
    pivot_signs,
    perturb,
    leaf_coupling,
    leaf_map,
    mid_front,
    level_map,
    top_front,
):
    depth_z = lax.axis_size("cube") // PLANE
    vmem = pl.BlockSpec(memory_space=pltpu.VMEM)
    dma = pltpu.SemaphoreType.DMA
    results = (
        jax.ShapeDtypeStruct((2, PIV, PIV), F32),
        jax.ShapeDtypeStruct((256, 256), F32),
        jax.ShapeDtypeStruct((512, 512), F32),
    )
    computed = pl.pallas_call(
        functools.partial(fused, depth_z),
        out_shape=results,
        in_specs=[vmem] * 11,
        out_specs=(vmem, vmem, vmem),
        scratch_shapes=[
            pltpu.VMEM((depth_z * SLOTS, PIV), F32),
            pltpu.VMEM((depth_z * SLOTS, PIV), F32),
            pltpu.VMEM((PLANE, 5, depth_z, PIV), F32),
            pltpu.VMEM((PLANE, 5, depth_z, PIV), F32),
            pltpu.VMEM((2560, 256), F32),
            pltpu.VMEM((512, 256), F32),
            pltpu.VMEM((2, 256, 256), F32),
            pltpu.VMEM((2, 3, PIV, PIV), F32),
            pltpu.VMEM((2, PIV, PIV), F32),
            pltpu.VMEM((2560, 256), F32),
            pltpu.VMEM((2560, 256), BF16),
            pltpu.VMEM((2560, 256), BF16),
            pltpu.VMEM((2560, 256), BF16),
            pltpu.VMEM((2560, 256), BF16),
            pltpu.VMEM((2, 512, 512), F32),
            pltpu.VMEM((512, 512), F32),
            pltpu.VMEM((4, 4, 2, 136, PIV), F32),
            pltpu.VMEM((512, 1024), BF16),
            pltpu.VMEM((1024, 512), BF16),
            pltpu.VMEM((1024, 512), BF16),
            dma((depth_z,)),
            dma((depth_z,)),
            dma((PLANE,)),
            dma((PLANE,)),
            dma((2 * HALF,)),
            dma((2 * HALF,)),
            dma((HALF,)),
            dma((HALF,)),
            dma((8,)),
            dma((8,)),
            dma((4,)),
            dma((2,)),
            dma((4,)),
            dma((2,)),
            dma((1,)),
            dma((1,)),
            dma((4,)),
            dma((2,)),
            dma((2,)),
            dma((15,)),
            dma((15,)),
        ],
        compiler_params=pltpu.CompilerParams(
            collective_id=0, has_side_effects=True, vmem_limit_bytes=56 * 1024 * 1024
        ),
    )(
        kkt_blocks,
        kkt_owner.reshape(1, -1),
        kkt_target,
        leaf_pivot,
        pivot_signs,
        perturb,
        leaf_coupling,
        leaf_map,
        mid_front,
        level_map,
        top_front,
    )
    return pl.pallas_call(
        hand_out,
        out_shape=results,
        in_specs=[vmem] * 3,
        out_specs=(vmem,) * 3,
    )(*computed)


def solution(mesh):
    in_specs = (
        P("front", "cube", None),
        P("front", "cube", None),
        P("front", "cube"),
        P("cube", "front", None),
        P("cube", "front"),
        P("cube", "front"),
        P("cube", "front", None),
        P("cube", "front"),
        P("cube", "front"),
        P(),
        P("cube", "front"),
    )
    out_specs = (P("cube", "front", None), P(("cube", "front"), None), P("cube", "front"))
    return jax.shard_map(local, mesh=mesh, in_specs=in_specs, out_specs=out_specs, check_vma=False)
```

```python
import functools

import jax
import jax.numpy as jnp
from jax import lax
from jax.experimental import pallas as pl
from jax.experimental.pallas import tpu as pltpu
from jax.sharding import PartitionSpec as P

PIV = 128
QUARTER = 512
PLANE = 8
SLOTS = 40
CHUNK = 32
HALF = 16
F32 = jnp.float32
BF16 = jnp.bfloat16
MESH = pl.DeviceIdType.MESH
NN = (((1,), (0,)), ((), ()))
NT = (((1,), (1,)), ((), ()))


def mm(a, b, dims=NN):
    return lax.dot_general(a, b, dims, preferred_element_type=F32)


def exact(a, b, dims=NN):
    return lax.dot_general(
        a, b, dims, precision=lax.Precision.HIGHEST, preferred_element_type=F32
    )


def halves(a):
    high = a.astype(BF16)
    return high, (a - high.astype(F32)).astype(BF16)


def dot3(a, b, dims=NN):
    a_high, a_low = halves(a)
    b_high, b_low = halves(b)
    return mm(a_high, b_high, dims) + (mm(a_high, b_low, dims) + mm(a_low, b_high, dims))


def iota(shape, axis):
    return lax.broadcasted_iota(jnp.int32, shape, axis)


def hits(a, b):
    return jnp.where(a == b, 1.0, 0.0).astype(BF16)


def newton_inverse(block):
    eye = iota((PIV, PIV), 0) == iota((PIV, PIV), 1)
    on_diagonal = jnp.where(eye, block, 0.0)
    by_col = 1.0 / jnp.sum(on_diagonal, axis=0, keepdims=True)
    by_row = 1.0 / jnp.sum(on_diagonal, axis=1, keepdims=True)
    current = jnp.where(eye, 2.0 * by_col, 0.0) - by_row * (block * by_col)
    return 2.0 * current - exact(current, exact(block, current))


def fused(
    depth_z,
    blocks,
    owner,
    target,
    leaf_pivot,
    signs,
    perturb,
    leaf_coupling,
    leaf_map,
    mid,
    level,
    top,
    factor_out,
    mid_factor_out,
    upper_out,
    s1,
    r1,
    s2,
    r2,
    rbuf,
    relay,
    piv,
    inv_sets,
    leaf_inv,
    lfull,
    l_high,
    l_low,
    p_high,
    p_low,
    vout,
    vin,
    kb,
    rt,
    kr_high,
    kr_low,
    zs,
    zr,
    ds,
    dr,
    ps,
    pr,
    gs,
    gr,
    hs,
    hr,
    us,
    ur,
    es,
    er,
    xs,
    xr,
    ts,
    vs,
    vr,
    ks,
    kr,
):
    cube = lax.axis_index("cube")
    front = lax.axis_index("front")
    pos_z = cube // PLANE
    pos_d = cube % PLANE
    low = cube % 2
    high = (cube // 2) % 2
    rho = 2 * low + high
    core_peer = cube + 1 - 2 * low
    y_peer = cube + 2 - 4 * high
    plane_base = cube - pos_d
    group = cube // 2
    row_count = blocks.shape[1]
    cube_count = depth_z * PLANE

    def at_z(step):
        return (pos_z + step) % depth_z

    def at_plane(step):
        return (pos_d + step) % PLANE

    barrier = pltpu.get_barrier_semaphore()

    def greet_z(step, carry):
        pl.semaphore_signal(
            barrier, inc=1, device_id=(at_z(step) * PLANE + pos_d, front), device_id_type=MESH
        )
        return carry

    def greet_plane(step, carry):
        pl.semaphore_signal(
            barrier, inc=1, device_id=(plane_base + at_plane(step), front), device_id_type=MESH
        )
        return carry

    lax.fori_loop(1, depth_z, greet_z, 0)
    lax.fori_loop(1, PLANE, greet_plane, 0)
    for step in range(1, 4):
        pl.semaphore_signal(
            barrier, inc=1, device_id=(cube, (front + step) % 4), device_id_type=MESH
        )

    @pl.when(front == 0)
    def _():
        rbuf[0:1024, :] = mid[:, 0:256].astype(F32)
        rbuf[1536:2048, :] = top[:, 0:256].astype(F32)

    own = owner[...]
    own_mask = iota((cube_count, row_count), 0) == own
    own_hits = jnp.where(own_mask, 1.0, 0.0).astype(BF16)
    before = jnp.where(
        iota((row_count, row_count), 0) < iota((row_count, row_count), 1), 1.0, 0.0
    ).astype(BF16)
    ahead = mm(own_hits, before)
    rank = jnp.sum(jnp.where(own_mask, ahead, 0.0), axis=0, keepdims=True).astype(jnp.int32)
    base = (own >> 3) * SLOTS + (own & 7)
    send_rows = depth_z * SLOTS
    row_ids = iota((send_rows, row_count), 0)
    to_slot = hits(row_ids, base + rank * PLANE)
    value_high, value_low = halves(blocks[0])
    marks = jnp.where(row_ids == base + 32, (target[...] + 1).astype(F32), 0.0).astype(BF16)
    by_rank = hits(iota((PIV, row_count), 0), rank)
    s1[...] = mm(to_slot, value_high) + mm(to_slot, value_low) + mm(marks, by_rank, NT)

    pl.semaphore_wait(barrier, depth_z + PLANE + 1)

    def z_copy(step):
        there = at_z(step)
        return pltpu.make_async_remote_copy(
            src_ref=s1.at[pl.ds(pl.multiple_of(there * SLOTS, 8), SLOTS)],
            dst_ref=r1.at[pl.ds(pl.multiple_of(pos_z * SLOTS, 8), SLOTS)],
            send_sem=zs.at[step],
            recv_sem=zr.at[step],
            device_id=(there * PLANE + pos_d, front),
            device_id_type=MESH,
        )

    def start_z(step, carry):
        z_copy(step).start()
        return carry

    lax.fori_loop(1, depth_z, start_z, 0)

    def chunk_copy(index, there):
        rows = pl.ds(pl.multiple_of(index * CHUNK, CHUNK), CHUNK)
        return pltpu.make_async_remote_copy(
            src_ref=rbuf.at[rows],
            dst_ref=rbuf.at[rows],
            send_sem=ps.at[index],
            recv_sem=pr.at[index],
            device_id=(cube, there),
            device_id_type=MESH,
        )

    up = (front + 1) % 4
    down = (front + 3) % 4
    holds_g = low == front // 2
    holds_u = rho == front
    col_g = pl.ds(1024, 512)
    col_u = pl.ds(2048, 512)
    first_g = pl.ds(pl.multiple_of((front % 2) * 512, 512), 512)
    pivot_g = pl.ds(0, 256)
    pivot_u = pl.ds(1536, 256)
    whole_u = pl.ds(1536, 512)

    def col_copy(part):
        start = (front % 2) * 512 + part * CHUNK
        return pltpu.make_async_remote_copy(
            src_ref=rbuf.at[pl.ds(pl.multiple_of(start, CHUNK), CHUNK)],
            dst_ref=rbuf.at[pl.ds(pl.multiple_of(1024 + part * CHUNK, CHUNK), CHUNK)],
            send_sem=gs.at[part],
            recv_sem=gr.at[part],
            device_id=(core_peer, front),
            device_id_type=MESH,
        )

    def pivot_copy(part):
        rows = pl.ds(pl.multiple_of(part * CHUNK, CHUNK), CHUNK)
        return pltpu.make_async_remote_copy(
            src_ref=rbuf.at[rows],
            dst_ref=piv.at[0, rows],
            send_sem=hs.at[part],
            recv_sem=hr.at[part],
            device_id=(core_peer, front),
            device_id_type=MESH,
        )

    def landed(index):
        @pl.when((low == 0) & (index < 8))
        def _():
            pivot_copy(index).start()

        @pl.when(holds_g & (index // HALF == front % 2))
        def _():
            col_copy(index % HALF).start()

    def upper_copy(half, there, number):
        rows = pl.ds(pl.multiple_of(1536 + 256 * half, 256), 256)
        return pltpu.make_async_remote_copy(
            src_ref=rbuf.at[rows],
            dst_ref=rbuf.at[rows],
            send_sem=us.at[number],
            recv_sem=ur.at[half],
            device_id=(cube, there),
            device_id_type=MESH,
        )

    def edge(source, place, number, arrival, there):
        return pltpu.make_async_remote_copy(
            src_ref=source,
            dst_ref=place,
            send_sem=es.at[number],
            recv_sem=er.at[arrival],
            device_id=(there, front),
            device_id_type=MESH,
        )

    def edge_col(number, there):
        return edge(rbuf.at[whole_u], rbuf.at[col_u], number, 0, there)

    def edge_col_on():
        return edge(rbuf.at[col_u], rbuf.at[col_u], 0, 0, core_peer)

    def edge_pivot(number, there):
        return edge(rbuf.at[pivot_u], piv.at[1], 2 + number, 1, there)

    def edge_pivot_on():
        return edge(piv.at[1], piv.at[1], 2, 1, core_peer)

    rho_y = rho + 1 - 2 * high

    def relay_copy():
        return pltpu.make_async_remote_copy(
            src_ref=rbuf.at[whole_u],
            dst_ref=relay,
            send_sem=xs.at[0],
            recv_sem=xr.at[0],
            device_id=(y_peer, front),
            device_id_type=MESH,
        )

    def relay_on():
        return pltpu.make_async_remote_copy(
            src_ref=relay,
            dst_ref=rbuf.at[col_u],
            send_sem=xs.at[0],
            recv_sem=er.at[0],
            device_id=(cube, rho_y),
            device_id_type=MESH,
        )

    def pivot_on(there):
        return pltpu.make_async_remote_copy(
            src_ref=piv.at[1],
            dst_ref=piv.at[1],
            send_sem=ts.at[there],
            recv_sem=er.at[1],
            device_id=(cube, there),
            device_id_type=MESH,
        )

    relays = (front == 0) & (rho != 0)
    relays_on = (front == 0) & (rho_y != 0)
    pivots_on = (front == 0) & (rho_y == 0)

    def start_edges():
        @pl.when(rho == 0)
        def _():
            edge_pivot(0, core_peer).start()

            @pl.when(front == 0)
            def _():
                edge_pivot(1, y_peer).start()

            piv[1] = rbuf[pivot_u, :]

        @pl.when(holds_u)
        def _():
            edge_col(0, core_peer).start()

            @pl.when(front == 0)
            def _():
                edge_col(1, y_peer).start()

            rbuf[col_u, :] = rbuf[whole_u, :]

    @pl.when(front == 0)
    def _():
        def push(index, carry):
            chunk_copy(index, up).start()
            chunk_copy(index + HALF, down).start()
            return carry

        lax.fori_loop(0, HALF, push, 0)

        def push_core(index, carry):
            landed(index)
            return carry

        lax.fori_loop(0, 2 * HALF, push_core, 0)
        upper_copy(0, 1, 0).start()
        upper_copy(1, 3, 3).start()
        upper_copy(1, 1, 2).start()
        upper_copy(0, 3, 1).start()
        start_edges()

    @pl.when(relays)
    def _():
        relay_copy().start()

    @pl.when(pivots_on)
    def _():
        edge_pivot(0, core_peer).wait_recv()
        edge_pivot_on().start()
        for there in (2, 1, 3):
            pivot_on(there).start()

    own_rows = pl.ds(pl.multiple_of(pos_z * SLOTS, 8), SLOTS)
    r1[own_rows, :] = s1[own_rows, :]

    eye = iota((PIV, PIV), 0) == iota((PIV, PIV), 1)
    links = level[pl.ds(group, 1), :]
    two_rows = iota((16, 2048), 0)
    digits = jnp.where(two_rows == 0, links >> 4, jnp.where(two_rows == 1, links & 15, 0))
    digits = digits.astype(F32).astype(BF16)

    def prepare_leaf(leaf, carry):
        shift = signs[pl.ds(leaf, 1), :].astype(F32) * perturb[pl.ds(leaf, 1), :]
        leaf_inv[leaf] = newton_inverse(leaf_pivot[leaf] + jnp.where(eye, shift, 0.0))
        picked = mm(digits, hits(iota((2048, PIV), 0), leaf_map[pl.ds(leaf, 1), :]))
        composite = picked[0:1, :] * 16.0 + picked[1:2, :]
        kb[0, front, leaf, 128:136, :] = jnp.broadcast_to(composite, (8, PIV))
        return carry

    lax.fori_loop(0, 2, prepare_leaf, 0)

    @pl.when((front == 1) | (front == 2))
    def _():
        def forward(index, carry):
            chunk_copy(index, up).wait_recv()
            chunk_copy(index, up).start()
            landed(index)

            @pl.when(front == 2)
            def _():
                chunk_copy(index + HALF, down).wait_recv()
                chunk_copy(index + HALF, down).start()
                landed(index + HALF)

            return carry

        lax.fori_loop(0, HALF, forward, 0)

    @pl.when(front == 3)
    def _():
        def forward(index, carry):
            chunk_copy(index + HALF, down).wait_recv()
            chunk_copy(index + HALF, down).start()
            landed(index + HALF)
            return carry

        lax.fori_loop(0, HALF, forward, 0)

    def wait_z(step, carry):
        z_copy(step).wait_recv()
        return carry

    lax.fori_loop(1, depth_z, wait_z, 0)
    for place in range(PLANE):
        for slot in range(5):
            s2[place, slot] = r1[pl.ds(slot * PLANE + place, depth_z, stride=SLOTS), :]

    def d_copy(step):
        there = at_plane(step)
        return pltpu.make_async_remote_copy(
            src_ref=s2.at[there],
            dst_ref=r2.at[pos_d],
            send_sem=ds.at[step],
            recv_sem=dr.at[step],
            device_id=(plane_base + there, front),
            device_id_type=MESH,
        )

    def start_d(step, carry):
        d_copy(step).start()
        return carry

    lax.fori_loop(1, PLANE, start_d, 0)
    r2[pos_d] = s2[pos_d]

    @pl.when(relays_on)
    def _():
        relay_copy().wait_recv()
        relay_on().start()

    @pl.when((front == 1) | (front == 3))
    def _():
        def take(index, carry):
            number = index + (HALF // 2) * (3 - front)
            chunk_copy(number, up).wait_recv()
            landed(number)
            return carry

        lax.fori_loop(0, HALF, take, 0)

    def invert_set(number, carry):
        rows_two = piv[number, 128:256, 0:128]
        first = newton_inverse(piv[number, 0:128, 0:128])
        second = newton_inverse(
            piv[number, 128:256, 128:256] - exact(exact(rows_two, first), rows_two, NT)
        )
        inv_sets[number, 0] = first
        inv_sets[number, 1] = second
        inv_sets[number, 2] = rows_two
        return carry

    @pl.when((front == 1) | (front == 3))
    def _():
        half_one = pl.ds(pl.multiple_of(1536 + 128 * (front - 1), 256), 256)
        passed = pltpu.make_async_remote_copy(
            src_ref=rbuf.at[half_one],
            dst_ref=rbuf.at[half_one],
            send_sem=us.at[0],
            recv_sem=ur.at[(front - 1) // 2],
            device_id=(cube, 2),
            device_id_type=MESH,
        )
        passed.wait_recv()
        passed.start()

    def wait_d(step, carry):
        d_copy(step).wait_recv()
        return carry

    lax.fori_loop(1, PLANE, wait_d, 0)

    slots_per = PLANE * depth_z
    marks_in = r2[:, 4].reshape(slots_per, PIV).T.astype(jnp.int32)
    arrivals = jnp.zeros((256, PIV), F32)
    for slot in range(4):
        to_row = hits(iota((256, slots_per), 0) + 1, marks_in[slot : slot + 1, :])
        got_high, got_low = halves(r2[:, slot].reshape(slots_per, PIV))
        arrivals = arrivals + mm(to_row, got_high) + mm(to_row, got_low)
    for leaf in range(2):
        coupling = leaf_coupling[leaf] + arrivals[leaf * PIV : (leaf + 1) * PIV, :]
        factor = exact(coupling, leaf_inv[leaf])
        factor_out[leaf] = factor
        kb[0, front, leaf, 0:128, :] = -exact(factor, coupling, NT)

    def k_copy(source, place, where, send, arrival, there):
        return pltpu.make_async_remote_copy(
            src_ref=kb.at[source, where],
            dst_ref=kb.at[place, where],
            send_sem=ks.at[send],
            recv_sem=kr.at[arrival],
            device_id=there,
            device_id_type=MESH,
        )

    def k_y():
        return k_copy(0, 2, front, 0, 0, (y_peer, front))

    def k_front(which, step):
        number = 1 + 3 * which + step - 1
        return k_copy(
            2 * which, 2 * which, front, number, number, (cube, (front + step) % 4)
        )

    def k_core(which, step):
        number = 7 + 4 * which + step
        return k_copy(
            2 * which,
            2 * which + 1,
            (front + 4 - step) % 4,
            number,
            number,
            (core_peer, front),
        )

    k_y().start()
    for step in (1, 3, 2):
        k_front(0, step).start()
    k_core(0, 0).start()

    @pl.when(low == 0)
    def _():
        piv[0] = rbuf[pivot_g, :]

    @pl.when(low != 0)
    def _():
        for part in range(8):
            pivot_copy(part).wait_recv()

    @pl.when(holds_g)
    def _():
        rbuf[col_g, :] = rbuf[first_g, :]

    lax.fori_loop(0, 1, invert_set, 0)

    def panel(index, carry):
        number = index // 3
        start = jnp.where(
            index < 2,
            low * 1024 + index * 512,
            jnp.where(index == 3, rho * 512, front * 512),
        )
        rows = pl.ds(pl.multiple_of(index * 512, 512), 512)
        place = iota((512, PIV), 0) + start
        first = rbuf[rows, 0:128]
        second = rbuf[rows, 128:256]
        past_one = place >= 128
        past_two = place >= 256
        lower_one = jnp.where(past_one, dot3(first, inv_sets[number, 0]), 0.0)
        second = second - dot3(lower_one, inv_sets[number, 2], NT)
        lower_two = jnp.where(past_two, dot3(second, inv_sets[number, 1]), 0.0)
        lfull[rows, 0:128] = lower_one
        lfull[rows, 128:256] = lower_two
        one_high, one_low = halves(lower_one)
        two_high, two_low = halves(lower_two)
        l_high[rows, 0:128] = one_high
        l_high[rows, 128:256] = two_high
        l_low[rows, 0:128] = one_low
        l_low[rows, 128:256] = two_low
        one_high, one_low = halves(jnp.where(past_one, first, 0.0))
        two_high, two_low = halves(jnp.where(past_two, second, 0.0))
        p_high[rows, 0:128] = one_high
        p_high[rows, 128:256] = two_high
        p_low[rows, 0:128] = one_low
        p_low[rows, 128:256] = two_low
        return carry

    lax.fori_loop(0, 2, panel, 0)

    @pl.when(low != front // 2)
    def _():
        for part in range(HALF):
            col_copy(part).wait_recv()

    lax.fori_loop(2, 3, panel, 0)

    def update(l_rows, p_rows):
        return mm(l_high[l_rows, :], p_high[p_rows, :], NT) + (
            mm(l_high[l_rows, :], p_low[p_rows, :], NT)
            + mm(l_low[l_rows, :], p_high[p_rows, :], NT)
        )

    def quarter_map(quarter):
        entries = level[pl.ds(group, 1), pl.ds(pl.multiple_of(quarter * 512, 512), 512)]
        kept = iota((1, 512), 1) + quarter * 512 >= 256
        return hits(iota((512, 512), 0), jnp.where(kept, entries - quarter * 512, -1))

    col_hits = quarter_map(front)

    def link(turn, carry):
        half = turn * high + (1 - turn) * (1 - high)
        rows = pl.ds(pl.multiple_of(half * 512, 512), 512)
        schur = mid[rows, :].astype(F32) - update(rows, col_g)
        s_high, s_low = halves(schur)
        t_high, t_low = halves(mm(s_high, col_hits, NT) + mm(s_low, col_hits, NT))
        row_hits = quarter_map(2 * low + half)
        vout[turn] = mm(row_hits, t_high) + mm(row_hits, t_low)
        return carry

    def v_copy(half):
        rows = pl.ds(256 * half, 256)
        return pltpu.make_async_remote_copy(
            src_ref=vout.at[0, rows],
            dst_ref=vin.at[rows],
            send_sem=vs.at[half],
            recv_sem=vr.at[half],
            device_id=(y_peer, front),
            device_id_type=MESH,
        )

    lax.fori_loop(0, 1, link, 0)
    @pl.when(rho != 1)
    def _():
        v_copy(0).start()

    v_copy(1).start()
    @pl.when((front == 1) | (front == 3))
    def _():
        upper_copy(1 - (front - 1) // 2, 1, 0).wait_recv()
        start_edges()


    mid_factor_out[...] = lfull[pl.ds(pl.multiple_of(front * 256, 256), 256), :]

    k_y().wait_recv()
    for step in (1, 3, 2):
        k_front(1, step).start()
    k_core(1, 0).start()
    lax.fori_loop(1, 2, link, 0)
    upper_out[...] = top[...].astype(F32) + vout[1]

    @pl.when(front == 2)
    def _():
        upper_copy(0, 1, 0).wait_recv()
        upper_copy(1, 1, 0).wait_recv()
        start_edges()

    ids = iota((512, PIV), 0)

    def gather_group(which, carry):
        def one(index, inner):
            entry = index // 2
            leaf = index % 2
            composite = kb[which, entry, leaf, 128:129, :].astype(jnp.int32)
            cols = pl.ds(pl.multiple_of(index * PIV, PIV), PIV)
            rt[:, cols] = hits(ids, composite - rho * 512)
            col_ids = hits(ids, composite - front * 512)
            k_high, k_low = halves(kb[which, entry, leaf, 0:128, :])
            spread_high, spread_low = halves(mm(k_high, col_ids, NT) + mm(k_low, col_ids, NT))
            kr_high[cols, :] = spread_high
            kr_low[cols, :] = spread_low
            return inner

        lax.fori_loop(0, 8, one, 0, unroll=True)
        upper_out[...] += mm(rt[...], kr_high[...]) + mm(rt[...], kr_low[...])
        return carry

    for step in (1, 3, 2):
        k_front(0, step).wait_recv()
        k_core(0, step).start()
        k_front(1, step).wait_recv()
        k_core(1, step).start()

    lax.fori_loop(0, 2, lambda turn, carry: gather_group(2 * turn, carry), 0)

    @pl.when((rho_y == 0) & (front != 0))
    def _():
        edge_pivot(0, core_peer).wait_recv()
        edge_pivot_on().start()

    @pl.when(rho_y == front)
    def _():
        edge_col(0, core_peer).wait_recv()
        edge_col_on().start()

    for step in range(4):
        k_core(0, step).wait_recv()
        k_core(1, step).wait_recv()
    lax.fori_loop(0, 2, lambda turn, carry: gather_group(2 * turn + 1, carry), 0)

    @pl.when((rho != 0) & (rho_y != 0))
    def _():
        edge_pivot(0, core_peer).wait_recv()

    lax.fori_loop(1, 2, invert_set, 0)
    lax.fori_loop(3, 4, panel, 0)

    @pl.when((rho != front) & (rho_y != front))
    def _():
        edge_col(0, core_peer).wait_recv()

    lax.fori_loop(4, 5, panel, 0)
    upper_out[...] += -update(whole_u, col_u)
    v_copy(1).wait_recv()
    upper_out[256:512, :] += vin[256:512, :]

    @pl.when(rho != 0)
    def _():
        v_copy(0).wait_recv()
        upper_out[0:256, :] += vin[0:256, :]

    def end_z(step, carry):
        z_copy(step).wait_send()
        return carry

    def end_d(step, carry):
        d_copy(step).wait_send()
        return carry

    lax.fori_loop(1, depth_z, end_z, 0)
    lax.fori_loop(1, PLANE, end_d, 0)

    @pl.when(front != 3)
    def _():
        def end_up(index, carry):
            chunk_copy(index, up).wait_send()
            return carry

        lax.fori_loop(0, HALF, end_up, 0)

    @pl.when(front != 1)
    def _():
        def end_down(index, carry):
            chunk_copy(index, down).wait_send()
            return carry

        lax.fori_loop(HALF, 2 * HALF, end_down, 0)

    @pl.when(low == 0)
    def _():
        for part in range(8):
            pivot_copy(part).wait_send()

    @pl.when(holds_g)
    def _():
        for part in range(HALF):
            col_copy(part).wait_send()

    @pl.when(front == 0)
    def _():
        for number in range(4):
            upper_copy(0, 1, number).wait_send()

    @pl.when((front == 1) | (front == 3))
    def _():
        upper_copy(0, 2, 0).wait_send()

    @pl.when(rho == 0)
    def _():
        edge_pivot(0, core_peer).wait_send()

        @pl.when(front == 0)
        def _():
            edge_pivot(1, y_peer).wait_send()

    @pl.when(rho_y == 0)
    def _():
        edge_pivot_on().wait_send()

    @pl.when(holds_u)
    def _():
        edge_col(0, core_peer).wait_send()

        @pl.when(front == 0)
        def _():
            edge_col(1, y_peer).wait_send()

    @pl.when(relays)
    def _():
        relay_copy().wait_send()

    @pl.when(relays_on)
    def _():
        relay_on().wait_send()

    @pl.when(pivots_on)
    def _():
        for there in (1, 2, 3):
            pivot_on(there).wait_send()

    @pl.when(rho_y == front)
    def _():
        edge_col_on().wait_send()

    v_copy(1).wait_send()

    @pl.when(rho != 1)
    def _():
        v_copy(0).wait_send()
    k_y().wait_send()
    for which in range(2):
        for step in range(1, 4):
            k_front(which, step).wait_send()
        for step in range(4):
            k_core(which, step).wait_send()


def hand_out(factor_in, mid_factor_in, upper_in, factor_out, mid_factor_out, upper_out):
    factor_out[...] = factor_in[...]
    mid_factor_out[...] = mid_factor_in[...]
    upper_out[...] = upper_in[...]


def local(
    kkt_blocks,
    kkt_owner,
    kkt_target,
    leaf_pivot,
    pivot_signs,
    perturb,
    leaf_coupling,
    leaf_map,
    mid_front,
    level_map,
    top_front,
):
    depth_z = lax.axis_size("cube") // PLANE
    vmem = pl.BlockSpec(memory_space=pltpu.VMEM)
    dma = pltpu.SemaphoreType.DMA
    results = (
        jax.ShapeDtypeStruct((2, PIV, PIV), F32),
        jax.ShapeDtypeStruct((256, 256), F32),
        jax.ShapeDtypeStruct((512, 512), F32),
    )
    computed = pl.pallas_call(
        functools.partial(fused, depth_z),
        out_shape=results,
        in_specs=[vmem] * 11,
        out_specs=(vmem, vmem, vmem),
        scratch_shapes=[
            pltpu.VMEM((depth_z * SLOTS, PIV), F32),
            pltpu.VMEM((depth_z * SLOTS, PIV), F32),
            pltpu.VMEM((PLANE, 5, depth_z, PIV), F32),
            pltpu.VMEM((PLANE, 5, depth_z, PIV), F32),
            pltpu.VMEM((2560, 256), F32),
            pltpu.VMEM((512, 256), F32),
            pltpu.VMEM((2, 256, 256), F32),
            pltpu.VMEM((2, 3, PIV, PIV), F32),
            pltpu.VMEM((2, PIV, PIV), F32),
            pltpu.VMEM((2560, 256), F32),
            pltpu.VMEM((2560, 256), BF16),
            pltpu.VMEM((2560, 256), BF16),
            pltpu.VMEM((2560, 256), BF16),
            pltpu.VMEM((2560, 256), BF16),
            pltpu.VMEM((2, 512, 512), F32),
            pltpu.VMEM((512, 512), F32),
            pltpu.VMEM((4, 4, 2, 136, PIV), F32),
            pltpu.VMEM((512, 1024), BF16),
            pltpu.VMEM((1024, 512), BF16),
            pltpu.VMEM((1024, 512), BF16),
            dma((depth_z,)),
            dma((depth_z,)),
            dma((PLANE,)),
            dma((PLANE,)),
            dma((2 * HALF,)),
            dma((2 * HALF,)),
            dma((HALF,)),
            dma((HALF,)),
            dma((8,)),
            dma((8,)),
            dma((4,)),
            dma((2,)),
            dma((4,)),
            dma((2,)),
            dma((1,)),
            dma((1,)),
            dma((4,)),
            dma((2,)),
            dma((2,)),
            dma((15,)),
            dma((15,)),
        ],
        compiler_params=pltpu.CompilerParams(
            collective_id=0, has_side_effects=True, vmem_limit_bytes=56 * 1024 * 1024
        ),
    )(
        kkt_blocks,
        kkt_owner.reshape(1, -1),
        kkt_target,
        leaf_pivot,
        pivot_signs,
        perturb,
        leaf_coupling,
        leaf_map,
        mid_front,
        level_map,
        top_front,
    )
    return pl.pallas_call(
        hand_out,
        out_shape=results,
        in_specs=[vmem] * 3,
        out_specs=(vmem,) * 3,
    )(*computed)


def solution(mesh):
    in_specs = (
        P("front", "cube", None),
        P("front", "cube", None),
        P("front", "cube"),
        P("cube", "front", None),
        P("cube", "front"),
        P("cube", "front"),
        P("cube", "front", None),
        P("cube", "front"),
        P("cube", "front"),
        P(),
        P("cube", "front"),
    )
    out_specs = (P("cube", "front", None), P(("cube", "front"), None), P("cube", "front"))
    return jax.shard_map(local, mesh=mesh, in_specs=in_specs, out_specs=out_specs, check_vma=False)
```
